512 devices in a mesh: exp: 16 (over y, core), space: 32 (over z, x).
Axes of the slice: x: 4, y: 8, z: 8, core: 2. Of those that a mesh axis runs over, the one named last changes fastest.
Arguments:
- initial: float32 [16, 4, 64, 64, 128], P('exp', None, 'space'), may hold values from -6 to 6
- cotangent: float32 [16, 4, 64, 64, 128], P('exp', None, 'space'), may hold values from -6 to 6
- permeability: float32 [64, 64, 128], P('space'), may hold values from 0.25 to 1.25
- labels: int32 [64, 64, 128], P('space'), may hold values from 0 to 511
- comp_scale: float32 [4], replicated, may hold values from 0.3 to 1
- coupling_mask: int32 [4, 4], replicated, may hold values from 0 to 1
- coupling_rate: float32 [4, 4], replicated, may hold values from 0.05 to 0.5
- dose: float32 [16], P('exp'), may hold values from 50 to 200
- inject_voxel: int32 [16], P('exp'), may hold values from 0 to 524287
- arrival: int32 [16], P('exp'), may hold values from 0 to 4
Outputs:
- concentration: float32 [16, 4, 64, 64, 128], P('exp', None, 'space')
- sensitivity: float32 [16, 4, 64, 64, 128], P('exp', None, 'space')
- perm_gradient: float32 [512], replicated
The draws below stay inside these ranges and needn't reach their ends.
All inputs are finite; a program needn't handle non-finite values.
Results may differ from the reference program's by a relative error of at most 0.0003.
Values sent between devices are 32-bit elements; how exact they have to be, the bound alone decides.
No kernel may reach another device: no remote copies, remote signals or barrier semaphores. Data moves between devices by JAX's collectives and lax.ppermute only.
A program may use at most 64 MiB of HBM per device.

```python
import math
import jax
import jax.numpy as jnp
from jax import lax

NY = 64
NZ = 128
COMP = 4
STEPS = 5
LABELS = 512
NX = 64
EXPERIMENTS = 16


def set_ends(array, key, least, largest):
    dims = array.shape
    spot = [jax.random.randint(jax.random.fold_in(key, axis), (), 0, dims[axis]) for axis in range(len(dims))]
    array = array.at[tuple(spot)].set(least)
    longest = dims.index(max(dims))
    spot[longest] = (spot[longest] + 1) % dims[longest]
    return array.at[tuple(spot)].set(largest)


def block_levels(rng, dims, pieces, least, top_value):
    gain = 1.0
    for dim, shards_of in pieces:
        draws = jax.random.uniform(jax.random.fold_in(jax.random.fold_in(rng, 6), dim), (shards_of,), jnp.float32, least / len(pieces), top_value / len(pieces))
        gain = gain * jnp.repeat(jnp.exp(draws), dims[dim] // shards_of).reshape((-1,) + (1,) * (len(dims) - 1 - dim))
    return gain


def gaussian(stream_key, dims, scale, most, pieces=(), held_as=jnp.bfloat16):
    drawn = scale * jax.random.normal(stream_key, dims, jnp.float32)
    if pieces:
        drawn = drawn * block_levels(stream_key, dims, pieces, -0.22, 0.18)
    return jnp.clip(drawn, -most, most).astype(held_as)


def setup_inputs(seed: int = 0) -> dict:
    key_of = jax.random.split(jax.random.key(seed), 11)
    initial = gaussian(key_of[0], (EXPERIMENTS, COMP, NX, NY, NZ), 1.0, 6.0, ((0, 16), (2, 32)), jnp.float32)
    cotangent = gaussian(key_of[1], (EXPERIMENTS, COMP, NX, NY, NZ), 1.0, 6.0, ((0, 16), (2, 32)), jnp.float32)
    permeability = jnp.clip(jnp.exp(math.log(1.25) - 1.609438 * jax.random.uniform(key_of[2], (NX, NY, NZ), jnp.float32) ** block_levels(key_of[2], (NX, NY, NZ), ((0, 32),), -0.2, 0.2)), 0.25, 1.25)
    labels = set_ends(jax.random.randint(key_of[3], (NX, NY, NZ), 0, LABELS), jax.random.fold_in(key_of[3], 1), 0, LABELS - 1).astype(jnp.int32)
    comp_scale = jnp.clip(jnp.exp(jax.random.uniform(key_of[4], (COMP,), jnp.float32, math.log(0.3), math.log(1.0))), 0.3, 1.0)
    coupling_mask = set_ends(jax.random.randint(key_of[5], (COMP, COMP), 0, 2), jax.random.fold_in(key_of[5], 1), 0, 1).astype(jnp.int32)
    coupling_rate = jnp.clip(jnp.exp(jax.random.uniform(key_of[6], (COMP, COMP), jnp.float32, math.log(0.05), math.log(0.5))), 0.05, 0.5)
    dose = jnp.clip(jnp.exp(math.log(200.0) - 1.3862944 * jax.random.uniform(key_of[7], (EXPERIMENTS,), jnp.float32) ** block_levels(key_of[7], (EXPERIMENTS,), ((0, 16),), -0.2, 0.2)), 50.0, 200.0)
    inject_voxel = set_ends(jax.random.randint(key_of[8], (EXPERIMENTS,), 0, NX * NY * NZ), jax.random.fold_in(key_of[8], 1), 0, (NX * NY * NZ) - 1).astype(jnp.int32)
    arrival = set_ends(jax.random.randint(key_of[9], (EXPERIMENTS,), 0, STEPS), jax.random.fold_in(key_of[9], 1), 0, STEPS - 1).astype(jnp.int32)
    return {"initial": initial, "cotangent": cotangent, "permeability": permeability, "labels": labels, "comp_scale": comp_scale, "coupling_mask": coupling_mask, "coupling_rate": coupling_rate, "dose": dose, "inject_voxel": inject_voxel, "arrival": arrival}


time_step = 0.1

def neighbors(field):
    lead = [(0, 0)] * (field.ndim - 3)
    pad = jnp.pad(field, lead + [(1, 1), (1, 1), (1, 1)])
    return [pad[..., 2:, 1:-1, 1:-1], pad[..., :-2, 1:-1, 1:-1], pad[..., 1:-1, 2:, 1:-1], pad[..., 1:-1, :-2, 1:-1], pad[..., 1:-1, 1:-1, 2:], pad[..., 1:-1, 1:-1, :-2]]

def laplace(field, perm):
    total = jnp.zeros_like(field)
    for near_u, near_k in zip(neighbors(field), neighbors(perm)):
        total = total + 0.5 * (perm + near_k) * (near_u - field)
    return total

def coupling(coupling_mask, coupling_rate):
    size = coupling_rate.shape[0]
    off = coupling_mask.astype(jnp.float32) * coupling_rate * (1.0 - jnp.eye(size, dtype=jnp.float32))
    return off - jnp.diag(lax.optimization_barrier(jnp.sum(off, axis=1)))

def run(perm, start, dose_one, voxel, arrive, comp_scale, mixing):
    cells = jnp.arange(NX * NY * NZ, dtype=jnp.int32).reshape(NX, NY, NZ)
    spot = (cells == voxel).astype(jnp.float32)
    state = start
    for step in range(STEPS):
        flow = comp_scale[:, None, None, None] * laplace(state, perm)
        flow = flow + jnp.einsum('cd,dxyz->cxyz', mixing, state, precision=lax.Precision.HIGHEST)
        pulse = jnp.where(step >= arrive, dose_one, 0.0) * time_step * spot
        state = state + time_step * flow
        state = state.at[0].add(pulse)
    return state

def reference(initial, cotangent, permeability, labels, comp_scale, coupling_mask, coupling_rate, dose, inject_voxel, arrival):
    mixing = coupling(coupling_mask, coupling_rate)

    def one(item):
        start, weight, dose_one, voxel, arrive = item
        final, pull = jax.vjp(lambda perm, first: run(perm, first, dose_one, voxel, arrive, comp_scale, mixing), permeability, start)
        grad_perm, grad_start = pull(weight)
        binned = jax.ops.segment_sum((grad_perm * permeability).reshape(-1), labels.reshape(-1), num_segments=LABELS)
        return (final, grad_start, binned)
    finals, sens, binned = lax.map(one, (initial, cotangent, dose, inject_voxel, arrival))
    total = lax.optimization_barrier(jnp.sum(binned, axis=0)) / math.sqrt(NX * NY * NZ * EXPERIMENTS / LABELS)
    return (finals, sens, total)
```

```python
import math

import jax
import jax.numpy as jnp
from jax import lax
from jax.experimental import pallas as pl
from jax.experimental.pallas import tpu as pltpu
from jax.sharding import PartitionSpec as P

STEPS = 5
LABELS = 512
TAU = 0.1
ROWS = 16
F32 = jnp.float32

A_AT, TS_AT, S_AT, LO_AT, HI_AT, DOSE_AT, NORM_AT = 0, 32, 36, 40, 41, 42, 43


def coupling(coupling_mask, coupling_rate):
    size = coupling_rate.shape[0]
    off = coupling_mask.astype(F32) * coupling_rate * (1.0 - jnp.eye(size, dtype=F32))
    return off - jnp.diag(jnp.sum(off, axis=1))


def up(ref, index, r, rows):
    if r + rows < ref.shape[-2]:
        return ref[(*index, pl.ds(r + 1, rows), slice(None))]
    return pltpu.roll(ref[(*index, pl.ds(r, rows), slice(None))], rows - 1, 0)


def down(ref, index, r, rows):
    if r > 0:
        return ref[(*index, pl.ds(r - 1, rows), slice(None))]
    return pltpu.roll(ref[(*index, pl.ds(r, rows), slice(None))], 1, 0)


def face_weights(planes, coef):
    wide, deep = coef.shape[-2:]
    row = lax.broadcasted_iota(jnp.int32, (wide, deep), 0)
    lane = lax.broadcasted_iota(jnp.int32, (wide, deep), 1)
    edges = (
        (row == 0).astype(F32)
        + (row == wide - 1).astype(F32)
        + (lane == 0).astype(F32)
        + (lane == deep - 1).astype(F32)
    )
    half = [0.5 * p for p in planes]
    for j in range(1, len(planes) - 1):
        h = half[j]
        zp = jnp.where(lane == deep - 1, 0.0, h + pltpu.roll(h, deep - 1, 1))
        yp = jnp.where(row == wide - 1, 0.0, h + pltpu.roll(h, wide - 1, 0))
        zm = pltpu.roll(zp, 1, 1)
        ym = pltpu.roll(yp, 1, 0)
        xp = h + half[j + 1]
        xm = h + half[j - 1]
        out = (zp, zm, yp, ym, xp, xm, zp + zm + yp + ym + xp + xm + edges * h)
        for k, value in enumerate(out):
            coef[j - 1, k] = value


def advance(f, step_of_u, get, put, coef, first, count, fl, it):
    wide, deep = coef.shape[-2:]
    offset = coef.shape[0] // 2 - 1
    for j in range(first, first + count):
        on = (f == 0) & (it[2] <= step_of_u) & (it[0] == j)
        amp = jnp.where(on, fl[DOSE_AT], 0.0)
        for r in range(0, wide, ROWS):
            rows = pl.ds(r, ROWS)
            zp, zm, yp, ym, xp, xm, total = [coef[j + offset, k, rows, :] for k in range(7)]
            center = []
            for c in range(4):
                ref, index = get(c, j)
                center.append(ref[(*index, rows, slice(None))])
            for c in range(4):
                ref, index = get(c, j)
                v = center[c]
                ref_up, index_up = get(c, j + 1)
                ref_dn, index_dn = get(c, j - 1)
                flow = zp * pltpu.roll(v, deep - 1, 1) + zm * pltpu.roll(v, 1, 1)
                flow = flow + (yp * up(ref, index, r, ROWS) + ym * down(ref, index, r, ROWS))
                flow = flow + (
                    xp * ref_up[(*index_up, rows, slice(None))]
                    + xm * ref_dn[(*index_dn, rows, slice(None))]
                )
                flow = flow - total * v
                new = fl[TS_AT + c] * flow
                for d in range(4):
                    new = new + fl[A_AT + f * 16 + c * 4 + d] * center[d]
                if c == 0:
                    at = (
                        lax.broadcasted_iota(jnp.int32, (ROWS, deep), 0) + r
                    ) * deep + lax.broadcasted_iota(jnp.int32, (ROWS, deep), 1)
                    new = new + jnp.where(at == it[1], amp, 0.0)
                if j < 0:
                    new = new * fl[LO_AT]
                if j > 1:
                    new = new * fl[HI_AT]
                out, index_out = put(c, j)
                out[(*index_out, rows, slice(None))] = new


def two_steps(first_step, perm_at):
    def kernel(fl, it, own, low, high, plow, pmid, phigh, mid, *rest):
        out, coef = rest[:-1], rest[-1]
        planes = [plow[(*perm_at, 0)], plow[(*perm_at, 1)], pmid[0], pmid[1]]
        planes += [phigh[(*perm_at, 0)], phigh[(*perm_at, 1)]]
        face_weights(planes, coef)

        def field(f, carry):
            def source(c, j):
                k = f * 4 + c
                if j < 0:
                    return low, (k, j + 2)
                if j > 1:
                    return high, (k, j - 2)
                return own, (k, j)

            def middle(c, j):
                return mid, (f * 4 + c, j + 1)

            def last(c, j):
                if len(out) == 1:
                    return out[0], (f * 4 + c, j)
                return out[j], (f * 4 + c,)

            advance(f, first_step, source, middle, coef, -1, 4, fl, it)
            advance(f, first_step + 1, middle, last, coef, 0, 2, fl, it)
            return carry

        lax.fori_loop(0, 2, field, 0)

    return kernel


def gradient(fl, s0, t1, s2, low2, high2, t3, s4a, s4b, out, fz, fy, fb):
    wide, deep = out.shape[-2:]

    def plane(stage, f, c, j):
        k = f * 4 + c
        if stage == 0:
            return s0, (k, j)
        if stage == 1:
            return t1, (k, j + 1)
        if stage == 3:
            return t3, (k, j + 1)
        if stage == 4:
            return (s4a, (k,)) if j == 0 else (s4b, (k,))
        if j < 0:
            return low2, (k, 1)
        if j > 1:
            return high2, (k, 0)
        return s2, (k, j)

    for r in range(0, wide, ROWS):
        rows = pl.ds(r, ROWS)
        x_low = x_mid = x_high = jnp.zeros((ROWS, deep), F32)
        acc_z, acc_y, acc_b = [[jnp.zeros((ROWS, deep), F32)] * 2 for _ in range(3)]
        for n in range(STEPS):
            for c in range(4):
                def load(f, j):
                    ref, index = plane(n if f == 0 else STEPS - 1 - n, f, c, j)
                    return ref[(*index, rows, slice(None))]

                def load_up(f, j):
                    ref, index = plane(n if f == 0 else STEPS - 1 - n, f, c, j)
                    return up(ref, index, r, ROWS)

                weight = fl[S_AT + c]
                u = [load(0, 0), load(0, 1)]
                l = [load(1, 0), load(1, 1)]
                w = [l[0] * weight, l[1] * weight]
                for j in range(2):
                    acc_b[j] = acc_b[j] + w[j] * u[j]
                    acc_z[j] = acc_z[j] + (pltpu.roll(w[j], deep - 1, 1) - w[j]) * (
                        pltpu.roll(u[j], deep - 1, 1) - u[j]
                    )
                    acc_y[j] = acc_y[j] + (load_up(1, j) * weight - w[j]) * (load_up(0, j) - u[j])
                x_mid = x_mid + (w[1] - w[0]) * (u[1] - u[0])
                if 0 < n < STEPS - 1:
                    x_low = x_low + (load(1, -1) * weight - w[0]) * (load(0, -1) - u[0])
                    x_high = x_high + (load(1, 2) * weight - w[1]) * (load(0, 2) - u[1])
        out[0, rows, :] = x_low + x_mid
        out[1, rows, :] = x_high + x_mid
        for j in range(2):
            fz[j, rows, :] = acc_z[j]
            fy[j, rows, :] = acc_y[j]
            fb[j, rows, :] = acc_b[j]
    row = lax.broadcasted_iota(jnp.int32, (wide, deep), 0)
    lane = lax.broadcasted_iota(jnp.int32, (wide, deep), 1)
    for j in range(2):
        b = fb[j]
        z, y = fz[j], fy[j]
        total = out[j] + jnp.where(lane == deep - 1, b, z)
        total = total + jnp.where(lane == 0, b, pltpu.roll(z, 1, 1))
        total = total + jnp.where(row == wide - 1, b, y)
        total = total + jnp.where(row == 0, b, pltpu.roll(y, 1, 0))
        out[j] = total


def final(fl, it, s0, low0, high0, s4a, s4b, low4, high4, part, perm, labels, conc, sens, bins, coef):
    wide, deep = perm.shape[-2:]
    face_weights([low0[8, 1], perm[0], perm[1], high0[8, 0]], coef)

    def bin_rows(k, total):
        r = pl.multiple_of(k * 8, 8)
        rows = pl.ds(r, 8)
        for j in range(2):
            g = part[j, rows, :]
            for c in range(4):
                weight = fl[S_AT + c]
                u4, l1 = (s4a, s4b)[j][c, rows, :], (s4a, s4b)[j][4 + c, rows, :]
                far = (low4, high4)[j]
                u0, l5 = s0[c, j, rows, :], s0[4 + c, j, rows, :]
                far0, at = ((low0, 1), (high0, 0))[j]
                g = g + weight * (
                    (far[4 + c, rows, :] - l1) * (far0[c, at, rows, :] - u0)
                    + (far0[4 + c, at, rows, :] - l5) * (far[c, rows, :] - u4)
                )
            value = g * perm[j, rows, :] * fl[NORM_AT]
            label = labels[j, rows, :]
            coarse, fine = label >> 5, label & 31
            left, right = [], []
            for i in range(8):
                spread = jnp.broadcast_to(coarse[i : i + 1], (16, deep))
                hit = spread == lax.broadcasted_iota(jnp.int32, (16, deep), 0)
                left.append(jnp.where(hit, jnp.broadcast_to(value[i : i + 1], (16, deep)), 0.0))
                spread = jnp.broadcast_to(fine[i : i + 1], (32, deep))
                hit = spread == lax.broadcasted_iota(jnp.int32, (32, deep), 0)
                right.append(hit.astype(F32))
            total = total + lax.dot_general(
                jnp.concatenate(left, axis=1),
                jnp.concatenate(right, axis=1),
                (((1,), (1,)), ((), ())),
                precision=lax.Precision.HIGHEST,
                preferred_element_type=F32,
            )
        return total

    bins[...] = lax.fori_loop(0, wide // 8, bin_rows, jnp.zeros((16, 32), F32))

    for f, out in ((0, conc), (1, sens)):
        def source(c, j):
            k = f * 4 + c
            return (low4, s4a, s4b, high4)[j + 1], (k,)

        def target(c, j):
            return out, (c, j)

        advance(f, STEPS - 1, source, target, coef, 0, 2, fl, it)


SMEM = pl.BlockSpec(memory_space=pltpu.SMEM)
VMEM = pl.BlockSpec(memory_space=pltpu.VMEM)


def call(kernel, ins, scalars, outs, scratch, name, flops):
    size = sum(math.prod(x.shape) for x in ins) + sum(math.prod(s) for s in outs)
    return pl.pallas_call(
        kernel,
        out_shape=[jax.ShapeDtypeStruct(s, F32) for s in outs],
        in_specs=[SMEM] * len(scalars) + [VMEM] * len(ins),
        out_specs=[VMEM] * len(outs),
        scratch_shapes=[pltpu.VMEM(s, F32) for s in scratch],
        compiler_params=pltpu.CompilerParams(vmem_limit_bytes=24 << 20),
        cost_estimate=pl.CostEstimate(flops=flops, bytes_accessed=4 * size, transcendentals=0),
        name=name,
    )(*scalars, *ins)


def neighbours(block_low, block_high):
    count = lax.axis_size("space")
    forward = [(i, i + 1) for i in range(count - 1)]
    backward = [(target, source) for source, target in forward]
    return lax.ppermute(block_high, "space", forward), lax.ppermute(block_low, "space", backward)


def sum_over(x, axis, groups):
    n = len(groups[0])
    copies = jnp.broadcast_to(x[None], (n, *x.shape))
    got = lax.all_to_all(copies, axis, 0, 0, axis_index_groups=groups, tiled=True)
    return jnp.sum(got, axis=0)


def on_device(
    initial,
    cotangent,
    permeability,
    labels,
    comp_scale,
    coupling_mask,
    coupling_rate,
    dose,
    inject_voxel,
    arrival,
):
    rows, wide, deep = permeability.shape
    spaces, exps = lax.axis_size("space"), lax.axis_size("exp")
    here = lax.axis_index("space")
    mixing = coupling(coupling_mask, coupling_rate)
    eye = jnp.eye(4, dtype=F32)
    norm = math.sqrt(rows * spaces * wide * deep * exps / LABELS)
    fl = jnp.concatenate(
        [
            (eye + TAU * mixing).reshape(-1),
            (eye + TAU * mixing.T).reshape(-1),
            TAU * comp_scale,
            comp_scale,
            jnp.stack([(here > 0).astype(F32), (here < spaces - 1).astype(F32)]),
            TAU * dose,
            jnp.full((1,), -0.5 * TAU / norm, F32),
        ]
    )
    voxel = inject_voxel[0]
    it = jnp.stack([voxel // (wide * deep) - here * rows, voxel % (wide * deep), arrival[0]])

    s0 = jnp.concatenate([initial[0], cotangent[0], permeability[None]], axis=0)
    low0, high0 = neighbours(s0, s0)
    slab, plane = (8, 2, wide, deep), (8, wide, deep)
    coef = (4, 7, wide, deep)
    t1, s2 = call(
        two_steps(0, (8,)), [s0, low0, high0, low0, permeability, high0], [fl, it],
        [(8, 4, wide, deep), slab], [coef], "steps_1_2", 20_000_000,
    )
    low2, high2 = neighbours(s2, s2)
    t3, s4a, s4b = call(
        two_steps(2, (8,)), [s2, low2, high2, low0, permeability, high0], [fl, it],
        [(8, 4, wide, deep), plane, plane], [coef], "steps_3_4", 20_000_000,
    )
    low4, high4 = neighbours(s4a, s4b)
    part, = call(
        gradient, [s0, t1, s2, low2, high2, t3, s4a, s4b], [fl],
        [(2, wide, deep)], [(2, wide, deep)] * 3, "gradient", 10_000_000,
    )
    conc, sens, bins = call(
        final, [s0, low0, high0, s4a, s4b, low4, high4, part, permeability, labels], [fl, it],
        [(4, 2, wide, deep), (4, 2, wide, deep), (16, 32)], [(2, 7, wide, deep)], "final", 20_000_000,
    )
    bins = sum_over(bins, "exp", [list(range(exps))])
    near = 8 if spaces % 8 == 0 else spaces
    bins = sum_over(bins, "space", [[g * near + i for i in range(near)] for g in range(spaces // near)])
    if spaces > near:
        bins = sum_over(bins, "space", [[g * near + i for g in range(spaces // near)] for i in range(near)])
    return conc[None], sens[None], bins.reshape(-1)


def solution(mesh):
    return jax.shard_map(
        on_device,
        mesh=mesh,
        in_specs=(
            P("exp", None, "space", None, None),
            P("exp", None, "space", None, None),
            P("space", None, None),
            P("space", None, None),
            P(),
            P(),
            P(),
            P("exp"),
            P("exp"),
            P("exp"),
        ),
        out_specs=(P("exp", None, "space", None, None), P("exp", None, "space", None, None), P()),
        check_vma=False,
    )
```

```python
import math

import jax
import jax.numpy as jnp
from jax import lax
from jax.experimental import pallas as pl
from jax.experimental.pallas import tpu as pltpu
from jax.sharding import PartitionSpec as P

STEPS = 5
LABELS = 512
TAU = 0.1
ROWS = 16
F32 = jnp.float32

A_AT, TS_AT, S_AT, LO_AT, HI_AT, DOSE_AT, NORM_AT = 0, 32, 36, 40, 41, 42, 43


def coupling(coupling_mask, coupling_rate):
    size = coupling_rate.shape[0]
    off = coupling_mask.astype(F32) * coupling_rate * (1.0 - jnp.eye(size, dtype=F32))
    return off - jnp.diag(jnp.sum(off, axis=1))


def up(ref, index, r, rows):
    if r + rows < ref.shape[-2]:
        return ref[(*index, pl.ds(r + 1, rows), slice(None))]
    return pltpu.roll(ref[(*index, pl.ds(r, rows), slice(None))], rows - 1, 0)


def down(ref, index, r, rows):
    if r > 0:
        return ref[(*index, pl.ds(r - 1, rows), slice(None))]
    return pltpu.roll(ref[(*index, pl.ds(r, rows), slice(None))], 1, 0)


def face_weights(planes, coef):
    wide, deep = coef.shape[-2:]
    row = lax.broadcasted_iota(jnp.int32, (wide, deep), 0)
    lane = lax.broadcasted_iota(jnp.int32, (wide, deep), 1)
    edges = (
        (row == 0).astype(F32)
        + (row == wide - 1).astype(F32)
        + (lane == 0).astype(F32)
        + (lane == deep - 1).astype(F32)
    )
    half = [0.5 * p for p in planes]
    for j in range(1, len(planes) - 1):
        h = half[j]
        zp = jnp.where(lane == deep - 1, 0.0, h + pltpu.roll(h, deep - 1, 1))
        yp = jnp.where(row == wide - 1, 0.0, h + pltpu.roll(h, wide - 1, 0))
        zm = pltpu.roll(zp, 1, 1)
        ym = pltpu.roll(yp, 1, 0)
        xp = h + half[j + 1]
        xm = h + half[j - 1]
        out = (zp, zm, yp, ym, xp, xm, zp + zm + yp + ym + xp + xm + edges * h)
        for k, value in enumerate(out):
            coef[j - 1, k] = value


def advance(f, step_of_u, get, put, coef, first, count, fl, it):
    wide, deep = coef.shape[-2:]
    offset = coef.shape[0] // 2 - 1
    for j in range(first, first + count):
        on = (f == 0) & (it[2] <= step_of_u) & (it[0] == j)
        amp = jnp.where(on, fl[DOSE_AT], 0.0)
        for r in range(0, wide, ROWS):
            rows = pl.ds(r, ROWS)
            zp, zm, yp, ym, xp, xm, total = [coef[j + offset, k, rows, :] for k in range(7)]
            center = []
            for c in range(4):
                ref, index = get(c, j)
                center.append(ref[(*index, rows, slice(None))])
            for c in range(4):
                ref, index = get(c, j)
                v = center[c]
                ref_up, index_up = get(c, j + 1)
                ref_dn, index_dn = get(c, j - 1)
                flow = zp * pltpu.roll(v, deep - 1, 1) + zm * pltpu.roll(v, 1, 1)
                flow = flow + (yp * up(ref, index, r, ROWS) + ym * down(ref, index, r, ROWS))
                flow = flow + (
                    xp * ref_up[(*index_up, rows, slice(None))]
                    + xm * ref_dn[(*index_dn, rows, slice(None))]
                )
                flow = flow - total * v
                new = fl[TS_AT + c] * flow
                for d in range(4):
                    new = new + fl[A_AT + f * 16 + c * 4 + d] * center[d]
                if c == 0:
                    at = (
                        lax.broadcasted_iota(jnp.int32, (ROWS, deep), 0) + r
                    ) * deep + lax.broadcasted_iota(jnp.int32, (ROWS, deep), 1)
                    new = new + jnp.where(at == it[1], amp, 0.0)
                if j < 0:
                    new = new * fl[LO_AT]
                if j > 1:
                    new = new * fl[HI_AT]
                out, index_out = put(c, j)
                out[(*index_out, rows, slice(None))] = new


def two_steps(first_step, perm_at):
    def kernel(fl, it, own, low, high, plow, pmid, phigh, mid, *rest):
        out, coef = rest[:-1], rest[-1]
        planes = [plow[(*perm_at, 0)], plow[(*perm_at, 1)], pmid[0], pmid[1]]
        planes += [phigh[(*perm_at, 0)], phigh[(*perm_at, 1)]]
        face_weights(planes, coef)

        def field(f, carry):
            def source(c, j):
                k = f * 4 + c
                if j < 0:
                    return low, (k, j + 2)
                if j > 1:
                    return high, (k, j - 2)
                return own, (k, j)

            def middle(c, j):
                return mid, (f * 4 + c, j + 1)

            def last(c, j):
                if len(out) == 1:
                    return out[0], (f * 4 + c, j)
                return out[j], (f * 4 + c,)

            advance(f, first_step, source, middle, coef, -1, 4, fl, it)
            advance(f, first_step + 1, middle, last, coef, 0, 2, fl, it)
            return carry

        lax.fori_loop(0, 2, field, 0)

    return kernel


def pieces(x):
    first = x.astype(jnp.bfloat16)
    rest = x - first.astype(F32)
    second = rest.astype(jnp.bfloat16)
    return first, second, (rest - second.astype(F32)).astype(jnp.bfloat16)


def gradient(fl, s0, low0, high0, t1, s2, low2, high2, t3, s4a, s4b, perm, labels, bins, out, fz, fy, fb, half):
    wide, deep = out.shape[-2:]

    def plane(stage, f, c, j):
        k = f * 4 + c
        if stage == 0:
            return s0, (k, j)
        if stage == 1:
            return t1, (k, j + 1)
        if stage == 3:
            return t3, (k, j + 1)
        if stage == 4:
            return (s4a, (k,)) if j == 0 else (s4b, (k,))
        if j < 0:
            return low2, (k, 1)
        if j > 1:
            return high2, (k, 0)
        return s2, (k, j)

    for r in range(0, wide, ROWS):
        rows = pl.ds(r, ROWS)
        x_low = x_mid = x_high = half_low = half_high = jnp.zeros((ROWS, deep), F32)
        acc_z, acc_y, acc_b = [[jnp.zeros((ROWS, deep), F32)] * 2 for _ in range(3)]
        for n in range(STEPS):
            for c in range(4):
                def load(f, j):
                    ref, index = plane(n if f == 0 else STEPS - 1 - n, f, c, j)
                    return ref[(*index, rows, slice(None))]

                def load_up(f, j):
                    ref, index = plane(n if f == 0 else STEPS - 1 - n, f, c, j)
                    return up(ref, index, r, ROWS)

                weight = fl[S_AT + c]
                u = [load(0, 0), load(0, 1)]
                l = [load(1, 0), load(1, 1)]
                w = [l[0] * weight, l[1] * weight]
                for j in range(2):
                    acc_b[j] = acc_b[j] + w[j] * u[j]
                    acc_z[j] = acc_z[j] + (pltpu.roll(w[j], deep - 1, 1) - w[j]) * (
                        pltpu.roll(u[j], deep - 1, 1) - u[j]
                    )
                    acc_y[j] = acc_y[j] + (load_up(1, j) * weight - w[j]) * (load_up(0, j) - u[j])
                x_mid = x_mid + (w[1] - w[0]) * (u[1] - u[0])
                if 0 < n < STEPS - 1:
                    x_low = x_low + (load(1, -1) * weight - w[0]) * (load(0, -1) - u[0])
                    x_high = x_high + (load(1, 2) * weight - w[1]) * (load(0, 2) - u[1])
                elif n == 0:
                    half_low = half_low + w[0] * (u[0] - low0[c, 1, rows, :])
                    half_high = half_high + w[1] * (u[1] - high0[c, 0, rows, :])
                else:
                    half_low = half_low + (w[0] - weight * low0[4 + c, 1, rows, :]) * u[0]
                    half_high = half_high + (w[1] - weight * high0[4 + c, 0, rows, :]) * u[1]
        out[0, rows, :] = x_low + x_mid + half_low
        out[1, rows, :] = x_high + x_mid + half_high
        half[0, rows, :] = half_low
        half[1, rows, :] = half_high
        for j in range(2):
            fz[j, rows, :] = acc_z[j]
            fy[j, rows, :] = acc_y[j]
            fb[j, rows, :] = acc_b[j]
    row = lax.broadcasted_iota(jnp.int32, (wide, deep), 0)
    lane = lax.broadcasted_iota(jnp.int32, (wide, deep), 1)
    for j in range(2):
        b = fb[j]
        z, y = fz[j], fy[j]
        total = out[j] + jnp.where(lane == deep - 1, b, z)
        total = total + jnp.where(lane == 0, b, pltpu.roll(z, 1, 1))
        total = total + jnp.where(row == wide - 1, b, y)
        total = total + jnp.where(row == 0, b, pltpu.roll(y, 1, 0))
        out[j] = total

    def bin_rows(k, total):
        rows = pl.ds(pl.multiple_of(k * 8, 8), 8)
        cells = [(out[j, rows, :], perm[j, rows, :], labels[j, rows, :]) for j in range(2)]
        for j, far, at in ((0, low0, 1), (1, high0, 0)):
            cells.append((half[j, rows, :], far[8, at, rows, :], far[9, at, rows, :].astype(jnp.int32)))
        left, right = [], []
        for g, weight, label in cells:
            value = g * weight * fl[NORM_AT]
            coarse, fine = ((label >> 5) & 3) * 4 + (label >> 7), label & 31
            for i in range(8):
                hit = jnp.broadcast_to(coarse[i : i + 1], (16, deep)) == lax.broadcasted_iota(
                    jnp.int32, (16, deep), 0
                )
                left.append(jnp.where(hit, jnp.broadcast_to(value[i : i + 1], (16, deep)), 0.0))
                hit = jnp.broadcast_to(fine[i : i + 1], (32, deep)) == lax.broadcasted_iota(
                    jnp.int32, (32, deep), 0
                )
                right.append(jnp.where(hit, 1.0, 0.0).astype(jnp.bfloat16))
        return total + lax.dot_general(
            jnp.concatenate(pieces(jnp.concatenate(left, axis=1)), axis=0),
            jnp.concatenate(right, axis=1),
            (((1,), (1,)), ((), ())),
            preferred_element_type=F32,
        )

    total = lax.fori_loop(0, wide // 8, bin_rows, jnp.zeros((48, 32), F32))
    total = total[0:16] + total[16:32] + total[32:48]
    for k in range(4):
        bins[:, 32 * k : 32 * k + 32] = total[4 * k : 4 * k + 4]


def last_step(fl, it, low0, perm, high0, low4, s4a, s4b, high4, conc, sens, coef):
    face_weights([low0[8, 1], perm[0], perm[1], high0[8, 0]], coef)
    for f, out in ((0, conc), (1, sens)):
        def source(c, j):
            return (low4, s4a, s4b, high4)[j + 1], (f * 4 + c,)

        def target(c, j):
            return out, (c, j)

        advance(f, STEPS - 1, source, target, coef, 0, 2, fl, it)


SMEM = pl.BlockSpec(memory_space=pltpu.SMEM)
VMEM = pl.BlockSpec(memory_space=pltpu.VMEM)


def call(kernel, ins, scalars, outs, scratch, name, flops):
    size = sum(math.prod(x.shape) for x in ins) + sum(math.prod(s) for s in outs)
    return pl.pallas_call(
        kernel,
        out_shape=[jax.ShapeDtypeStruct(s, F32) for s in outs],
        in_specs=[SMEM] * len(scalars) + [VMEM] * len(ins),
        out_specs=[VMEM] * len(outs),
        scratch_shapes=[pltpu.VMEM(s, F32) for s in scratch],
        compiler_params=pltpu.CompilerParams(vmem_limit_bytes=24 << 20),
        cost_estimate=pl.CostEstimate(flops=flops, bytes_accessed=4 * size, transcendentals=0),
        name=name,
    )(*scalars, *ins)


def neighbours(block_low, block_high):
    count = lax.axis_size("space")
    forward = [(i, i + 1) for i in range(count - 1)]
    backward = [(target, source) for source, target in forward]
    return lax.ppermute(block_high, "space", forward), lax.ppermute(block_low, "space", backward)


def sum_over(x, axis, groups):
    n = len(groups[0])
    copies = jnp.broadcast_to(x[None], (n, *x.shape))
    got = lax.all_to_all(copies, axis, 0, 0, axis_index_groups=groups, tiled=True)
    return jnp.sum(got, axis=0)


def on_device(
    initial,
    cotangent,
    permeability,
    labels,
    comp_scale,
    coupling_mask,
    coupling_rate,
    dose,
    inject_voxel,
    arrival,
):
    rows, wide, deep = permeability.shape
    spaces, exps = lax.axis_size("space"), lax.axis_size("exp")
    here = lax.axis_index("space")
    mixing = coupling(coupling_mask, coupling_rate)
    eye = jnp.eye(4, dtype=F32)
    norm = math.sqrt(rows * spaces * wide * deep * exps / LABELS)
    fl = jnp.concatenate(
        [
            (eye + TAU * mixing).reshape(-1),
            (eye + TAU * mixing.T).reshape(-1),
            TAU * comp_scale,
            comp_scale,
            jnp.stack([(here > 0).astype(F32), (here < spaces - 1).astype(F32)]),
            TAU * dose,
            jnp.full((1,), -0.5 * TAU / norm, F32),
        ]
    )
    voxel = inject_voxel[0]
    it = jnp.stack([voxel // (wide * deep) - here * rows, voxel % (wide * deep), arrival[0]])

    s0 = jnp.concatenate([initial[0], cotangent[0], permeability[None], labels.astype(F32)[None]], axis=0)
    low0, high0 = neighbours(s0, s0)
    slab, plane = (8, 2, wide, deep), (8, wide, deep)
    coef = (4, 7, wide, deep)
    t1, s2 = call(
        two_steps(0, (8,)), [s0, low0, high0, low0, permeability, high0], [fl, it],
        [(8, 4, wide, deep), slab], [coef], "steps_1_2", 20_000_000,
    )
    low2, high2 = neighbours(s2, s2)
    t3, s4a, s4b = call(
        two_steps(2, (8,)), [s2, low2, high2, low0, permeability, high0], [fl, it],
        [(8, 4, wide, deep), plane, plane], [coef], "steps_3_4", 20_000_000,
    )
    low4, high4 = neighbours(s4a, s4b)
    bins, = call(
        gradient, [s0, low0, high0, t1, s2, low2, high2, t3, s4a, s4b, permeability, labels], [fl],
        [(4, 128)], [(2, wide, deep)] * 5, "gradient", 20_000_000,
    )
    conc, sens = call(
        last_step, [low0, permeability, high0, low4, s4a, s4b, high4], [fl, it],
        [(4, 2, wide, deep)] * 2, [(2, 7, wide, deep)], "step_5", 10_000_000,
    )
    bins = sum_over(bins, "exp", [list(range(exps))])
    near = 8 if spaces % 8 == 0 else spaces
    bins = sum_over(bins, "space", [[g * near + i for i in range(near)] for g in range(spaces // near)])
    if spaces > near:
        bins = sum_over(bins, "space", [[g * near + i for g in range(spaces // near)] for i in range(near)])
    return conc[None], sens[None], bins.reshape(-1)


def solution(mesh):
    return jax.shard_map(
        on_device,
        mesh=mesh,
        in_specs=(
            P("exp", None, "space", None, None),
            P("exp", None, "space", None, None),
            P("space", None, None),
            P("space", None, None),
            P(),
            P(),
            P(),
            P("exp"),
            P("exp"),
            P("exp"),
        ),
        out_specs=(P("exp", None, "space", None, None), P("exp", None, "space", None, None), P()),
        check_vma=False,
    )
```

```python
import math

import jax
import jax.numpy as jnp
from jax import lax
from jax.experimental import pallas as pl
from jax.experimental.pallas import tpu as pltpu
from jax.sharding import PartitionSpec as P

STEPS = 5
LABELS = 512
TAU = 0.1
ROWS = 16
F32 = jnp.float32

A_AT, TS_AT, S_AT, LO_AT, HI_AT, DOSE_AT, NORM_AT = 0, 32, 36, 40, 41, 42, 43


def coupling(coupling_mask, coupling_rate):
    size = coupling_rate.shape[0]
    off = coupling_mask.astype(F32) * coupling_rate * (1.0 - jnp.eye(size, dtype=F32))
    return off - jnp.diag(jnp.sum(off, axis=1))


def up(ref, index, r, rows):
    if r + rows < ref.shape[-2]:
        return ref[(*index, pl.ds(r + 1, rows), slice(None))]
    return pltpu.roll(ref[(*index, pl.ds(r, rows), slice(None))], rows - 1, 0)


def down(ref, index, r, rows):
    if r > 0:
        return ref[(*index, pl.ds(r - 1, rows), slice(None))]
    return pltpu.roll(ref[(*index, pl.ds(r, rows), slice(None))], 1, 0)


def face_weights(planes, coef):
    wide, deep = coef.shape[-2:]
    row = lax.broadcasted_iota(jnp.int32, (wide, deep), 0)
    lane = lax.broadcasted_iota(jnp.int32, (wide, deep), 1)
    edges = (
        (row == 0).astype(F32)
        + (row == wide - 1).astype(F32)
        + (lane == 0).astype(F32)
        + (lane == deep - 1).astype(F32)
    )
    half = [0.5 * p for p in planes]
    for j in range(1, len(planes) - 1):
        h = half[j]
        zp = jnp.where(lane == deep - 1, 0.0, h + pltpu.roll(h, deep - 1, 1))
        yp = jnp.where(row == wide - 1, 0.0, h + pltpu.roll(h, wide - 1, 0))
        zm = pltpu.roll(zp, 1, 1)
        ym = pltpu.roll(yp, 1, 0)
        xp = h + half[j + 1]
        xm = h + half[j - 1]
        out = (zp, zm, yp, ym, xp, xm, zp + zm + yp + ym + xp + xm + edges * h)
        for k, value in enumerate(out):
            coef[j - 1, k] = value


def advance(f, step_of_u, get, put, coef, first, count, fl, it):
    wide, deep = coef.shape[-2:]
    offset = coef.shape[0] // 2 - 1
    for j in range(first, first + count):
        on = (f == 0) & (it[2] <= step_of_u) & (it[0] == j)
        amp = jnp.where(on, fl[DOSE_AT], 0.0)
        for r in range(0, wide, ROWS):
            rows = pl.ds(r, ROWS)
            zp, zm, yp, ym, xp, xm, total = [coef[j + offset, k, rows, :] for k in range(7)]
            center = []
            for c in range(4):
                ref, index = get(c, j)
                center.append(ref[(*index, rows, slice(None))])
            for c in range(4):
                ref, index = get(c, j)
                v = center[c]
                ref_up, index_up = get(c, j + 1)
                ref_dn, index_dn = get(c, j - 1)
                flow = zp * pltpu.roll(v, deep - 1, 1) + zm * pltpu.roll(v, 1, 1)
                flow = flow + (yp * up(ref, index, r, ROWS) + ym * down(ref, index, r, ROWS))
                flow = flow + (
                    xp * ref_up[(*index_up, rows, slice(None))]
                    + xm * ref_dn[(*index_dn, rows, slice(None))]
                )
                flow = flow - total * v
                new = fl[TS_AT + c] * flow
                for d in range(4):
                    new = new + fl[A_AT + f * 16 + c * 4 + d] * center[d]
                if c == 0:
                    at = (
                        lax.broadcasted_iota(jnp.int32, (ROWS, deep), 0) + r
                    ) * deep + lax.broadcasted_iota(jnp.int32, (ROWS, deep), 1)
                    new = new + jnp.where(at == it[1], amp, 0.0)
                if j < 0:
                    new = new * fl[LO_AT]
                if j > 1:
                    new = new * fl[HI_AT]
                out, index_out = put(c, j)
                out[(*index_out, rows, slice(None))] = new


def two_steps(first_step, perm_at):
    def kernel(fl, it, own, low, high, plow, pmid, phigh, *rest):
        labels, rest = (rest[:1], rest[1:]) if first_step == 0 else ((), rest)
        mid, out, coef = rest[0], rest[1:-1], rest[-1]
        for ref in labels:
            out[0][8] = ref[...].astype(F32)
        planes = [plow[(*perm_at, 0)], plow[(*perm_at, 1)], pmid[0], pmid[1]]
        planes += [phigh[(*perm_at, 0)], phigh[(*perm_at, 1)]]
        face_weights(planes, coef)

        def field(f, carry):
            def source(c, j):
                k = f * 4 + c
                if j < 0:
                    return low, (k, j + 2)
                if j > 1:
                    return high, (k, j - 2)
                return own, (k, j)

            def middle(c, j):
                return mid, (f * 4 + c, j + 1)

            def last(c, j):
                if len(out) == 1:
                    return out[0], (f * 4 + c, j)
                return out[j], (f * 4 + c,)

            advance(f, first_step, source, middle, coef, -1, 4, fl, it)
            advance(f, first_step + 1, middle, last, coef, 0, 2, fl, it)
            return carry

        lax.fori_loop(0, 2, field, 0)

    return kernel


def pieces(x):
    first = x.astype(jnp.bfloat16)
    rest = x - first.astype(F32)
    second = rest.astype(jnp.bfloat16)
    return first, second, (rest - second.astype(F32)).astype(jnp.bfloat16)


def gradient(fl, s0, low0, high0, t1, s2, low2, high2, t3, s4a, s4b, perm, labels, bins, out, fz, fy, fb, half):
    wide, deep = out.shape[-2:]

    def plane(stage, f, c, j):
        k = f * 4 + c
        if stage == 0:
            return s0, (k, j)
        if stage == 1:
            return t1, (k, j + 1)
        if stage == 3:
            return t3, (k, j + 1)
        if stage == 4:
            return (s4a, (k,)) if j == 0 else (s4b, (k,))
        if j < 0:
            return low2, (k, 1)
        if j > 1:
            return high2, (k, 0)
        return s2, (k, j)

    for r in range(0, wide, ROWS):
        rows = pl.ds(r, ROWS)
        x_low = x_mid = x_high = half_low = half_high = jnp.zeros((ROWS, deep), F32)
        acc_z, acc_y, acc_b = [[jnp.zeros((ROWS, deep), F32)] * 2 for _ in range(3)]
        for n in range(STEPS):
            for c in range(4):
                def load(f, j):
                    ref, index = plane(n if f == 0 else STEPS - 1 - n, f, c, j)
                    return ref[(*index, rows, slice(None))]

                def load_up(f, j):
                    ref, index = plane(n if f == 0 else STEPS - 1 - n, f, c, j)
                    return up(ref, index, r, ROWS)

                weight = fl[S_AT + c]
                u = [load(0, 0), load(0, 1)]
                l = [load(1, 0), load(1, 1)]
                w = [l[0] * weight, l[1] * weight]
                for j in range(2):
                    acc_b[j] = acc_b[j] + w[j] * u[j]
                    acc_z[j] = acc_z[j] + (pltpu.roll(w[j], deep - 1, 1) - w[j]) * (
                        pltpu.roll(u[j], deep - 1, 1) - u[j]
                    )
                    acc_y[j] = acc_y[j] + (load_up(1, j) * weight - w[j]) * (load_up(0, j) - u[j])
                x_mid = x_mid + (w[1] - w[0]) * (u[1] - u[0])
                if 0 < n < STEPS - 1:
                    x_low = x_low + (load(1, -1) * weight - w[0]) * (load(0, -1) - u[0])
                    x_high = x_high + (load(1, 2) * weight - w[1]) * (load(0, 2) - u[1])
                elif n == 0:
                    half_low = half_low + w[0] * (u[0] - low0[c, 1, rows, :])
                    half_high = half_high + w[1] * (u[1] - high0[c, 0, rows, :])
                else:
                    half_low = half_low + (w[0] - weight * low0[4 + c, 1, rows, :]) * u[0]
                    half_high = half_high + (w[1] - weight * high0[4 + c, 0, rows, :]) * u[1]
        out[0, rows, :] = x_low + x_mid + half_low
        out[1, rows, :] = x_high + x_mid + half_high
        half[0, rows, :] = half_low
        half[1, rows, :] = half_high
        for j in range(2):
            fz[j, rows, :] = acc_z[j]
            fy[j, rows, :] = acc_y[j]
            fb[j, rows, :] = acc_b[j]
    row = lax.broadcasted_iota(jnp.int32, (wide, deep), 0)
    lane = lax.broadcasted_iota(jnp.int32, (wide, deep), 1)
    for j in range(2):
        b = fb[j]
        z, y = fz[j], fy[j]
        total = out[j] + jnp.where(lane == deep - 1, b, z)
        total = total + jnp.where(lane == 0, b, pltpu.roll(z, 1, 1))
        total = total + jnp.where(row == wide - 1, b, y)
        total = total + jnp.where(row == 0, b, pltpu.roll(y, 1, 0))
        out[j] = total

    def bin_rows(k, total):
        rows = pl.ds(pl.multiple_of(k * 8, 8), 8)
        cells = [(out[j, rows, :], perm[j, rows, :], labels[j, rows, :]) for j in range(2)]
        for j, far, names, at in ((0, low0, low2, 1), (1, high0, high2, 0)):
            cells.append((half[j, rows, :], far[8, at, rows, :], names[8, at, rows, :].astype(jnp.int32)))
        left, right = [], []
        for g, weight, label in cells:
            value = g * weight * fl[NORM_AT]
            coarse, fine = ((label >> 5) & 3) * 4 + (label >> 7), label & 31
            for i in range(8):
                hit = jnp.broadcast_to(coarse[i : i + 1], (16, deep)) == lax.broadcasted_iota(
                    jnp.int32, (16, deep), 0
                )
                left.append(jnp.where(hit, jnp.broadcast_to(value[i : i + 1], (16, deep)), 0.0))
                hit = jnp.broadcast_to(fine[i : i + 1], (32, deep)) == lax.broadcasted_iota(
                    jnp.int32, (32, deep), 0
                )
                right.append(jnp.where(hit, 1.0, 0.0).astype(jnp.bfloat16))
        return total + lax.dot_general(
            jnp.concatenate(pieces(jnp.concatenate(left, axis=1)), axis=0),
            jnp.concatenate(right, axis=1),
            (((1,), (1,)), ((), ())),
            preferred_element_type=F32,
        )

    total = lax.fori_loop(0, wide // 8, bin_rows, jnp.zeros((48, 32), F32))
    total = total[0:16] + total[16:32] + total[32:48]
    for k in range(4):
        bins[:, 32 * k : 32 * k + 32] = total[4 * k : 4 * k + 4]


def last_step(fl, it, low0, perm, high0, low4, s4a, s4b, high4, conc, sens, coef):
    face_weights([low0[8, 1], perm[0], perm[1], high0[8, 0]], coef)
    for f, out in ((0, conc), (1, sens)):
        def source(c, j):
            return (low4, s4a, s4b, high4)[j + 1], (f * 4 + c,)

        def target(c, j):
            return out, (c, j)

        advance(f, STEPS - 1, source, target, coef, 0, 2, fl, it)


SMEM = pl.BlockSpec(memory_space=pltpu.SMEM)
VMEM = pl.BlockSpec(memory_space=pltpu.VMEM)


def call(kernel, ins, scalars, outs, scratch, name, flops):
    size = sum(math.prod(x.shape) for x in ins) + sum(math.prod(s) for s in outs)
    return pl.pallas_call(
        kernel,
        out_shape=[jax.ShapeDtypeStruct(s, F32) for s in outs],
        in_specs=[SMEM] * len(scalars) + [VMEM] * len(ins),
        out_specs=[VMEM] * len(outs),
        scratch_shapes=[pltpu.VMEM(s, F32) for s in scratch],
        compiler_params=pltpu.CompilerParams(vmem_limit_bytes=24 << 20),
        cost_estimate=pl.CostEstimate(flops=flops, bytes_accessed=4 * size, transcendentals=0),
        name=name,
    )(*scalars, *ins)


def neighbours(block_low, block_high):
    count = lax.axis_size("space")
    forward = [(i, i + 1) for i in range(count - 1)]
    backward = [(target, source) for source, target in forward]
    return lax.ppermute(block_high, "space", forward), lax.ppermute(block_low, "space", backward)


def sum_over(x, axis, groups):
    n = len(groups[0])
    copies = jnp.broadcast_to(x[None], (n, *x.shape))
    got = lax.all_to_all(copies, axis, 0, 0, axis_index_groups=groups, tiled=True)
    return jnp.sum(got, axis=0)


def on_device(
    initial,
    cotangent,
    permeability,
    labels,
    comp_scale,
    coupling_mask,
    coupling_rate,
    dose,
    inject_voxel,
    arrival,
):
    rows, wide, deep = permeability.shape
    spaces, exps = lax.axis_size("space"), lax.axis_size("exp")
    here = lax.axis_index("space")
    mixing = coupling(coupling_mask, coupling_rate)
    eye = jnp.eye(4, dtype=F32)
    norm = math.sqrt(rows * spaces * wide * deep * exps / LABELS)
    fl = jnp.concatenate(
        [
            (eye + TAU * mixing).reshape(-1),
            (eye + TAU * mixing.T).reshape(-1),
            TAU * comp_scale,
            comp_scale,
            jnp.stack([(here > 0).astype(F32), (here < spaces - 1).astype(F32)]),
            TAU * dose,
            jnp.full((1,), -0.5 * TAU / norm, F32),
        ]
    )
    voxel = inject_voxel[0]
    it = jnp.stack([voxel // (wide * deep) - here * rows, voxel % (wide * deep), arrival[0]])

    s0 = jnp.concatenate([initial[0], cotangent[0], permeability[None]], axis=0)
    low0, high0 = neighbours(s0, s0)
    plane = (8, wide, deep)
    coef = (4, 7, wide, deep)
    t1, s2 = call(
        two_steps(0, (8,)), [s0, low0, high0, low0, permeability, high0, labels], [fl, it],
        [(8, 4, wide, deep), (9, 2, wide, deep)], [coef], "steps_1_2", 20_000_000,
    )
    low2, high2 = neighbours(s2, s2)
    t3, s4a, s4b = call(
        two_steps(2, (8,)), [s2, low2, high2, low0, permeability, high0], [fl, it],
        [(8, 4, wide, deep), plane, plane], [coef], "steps_3_4", 20_000_000,
    )
    bins, = call(
        gradient, [s0, low0, high0, t1, s2, low2, high2, t3, s4a, s4b, permeability, labels], [fl],
        [(4, 128)], [(2, wide, deep)] * 5, "gradient", 20_000_000,
    )
    near = 4 if spaces % 4 == 0 else spaces
    bins = sum_over(bins, "space", [[g * near + i for i in range(near)] for g in range(spaces // near)])
    if spaces > near:
        bins = sum_over(bins, "space", [[g * near + i for g in range(spaces // near)] for i in range(near)])
    bins, last_low, last_high = lax.optimization_barrier((bins, s4a, s4b))
    low4, high4 = neighbours(last_low, last_high)
    conc, sens = call(
        last_step, [low0, permeability, high0, low4, s4a, s4b, high4], [fl, it],
        [(4, 2, wide, deep)] * 2, [(2, 7, wide, deep)], "step_5", 10_000_000,
    )
    bins = sum_over(bins, "exp", [list(range(exps))])
    return conc[None], sens[None], bins.reshape(-1)


def solution(mesh):
    return jax.shard_map(
        on_device,
        mesh=mesh,
        in_specs=(
            P("exp", None, "space", None, None),
            P("exp", None, "space", None, None),
            P("space", None, None),
            P("space", None, None),
            P(),
            P(),
            P(),
            P("exp"),
            P("exp"),
            P("exp"),
        ),
        out_specs=(P("exp", None, "space", None, None), P("exp", None, "space", None, None), P()),
        check_vma=False,
    )
```

```python
import math

import jax
import jax.numpy as jnp
from jax import lax
from jax.experimental import pallas as pl
from jax.experimental.pallas import tpu as pltpu
from jax.sharding import PartitionSpec as P

STEPS = 5
LABELS = 512
TAU = 0.1
ROWS = 16
F32 = jnp.float32

A_AT, TS_AT, S_AT, LO_AT, HI_AT, DOSE_AT, NORM_AT = 0, 32, 36, 40, 41, 42, 43


def coupling(coupling_mask, coupling_rate):
    size = coupling_rate.shape[0]
    off = coupling_mask.astype(F32) * coupling_rate * (1.0 - jnp.eye(size, dtype=F32))
    return off - jnp.diag(jnp.sum(off, axis=1))


def up(ref, index, r, rows):
    if r + rows < ref.shape[-2]:
        return ref[(*index, pl.ds(r + 1, rows), slice(None))]
    return pltpu.roll(ref[(*index, pl.ds(r, rows), slice(None))], rows - 1, 0)


def down(ref, index, r, rows):
    if r > 0:
        return ref[(*index, pl.ds(r - 1, rows), slice(None))]
    return pltpu.roll(ref[(*index, pl.ds(r, rows), slice(None))], 1, 0)


def face_weights(planes, coef):
    wide, deep = coef.shape[-2:]
    row = lax.broadcasted_iota(jnp.int32, (wide, deep), 0)
    lane = lax.broadcasted_iota(jnp.int32, (wide, deep), 1)
    edges = (
        (row == 0).astype(F32)
        + (row == wide - 1).astype(F32)
        + (lane == 0).astype(F32)
        + (lane == deep - 1).astype(F32)
    )
    half = [0.5 * p for p in planes]
    for j in range(1, len(planes) - 1):
        h = half[j]
        zp = jnp.where(lane == deep - 1, 0.0, h + pltpu.roll(h, deep - 1, 1))
        yp = jnp.where(row == wide - 1, 0.0, h + pltpu.roll(h, wide - 1, 0))
        zm = pltpu.roll(zp, 1, 1)
        ym = pltpu.roll(yp, 1, 0)
        xp = h + half[j + 1]
        xm = h + half[j - 1]
        out = (zp, zm, yp, ym, xp, xm, zp + zm + yp + ym + xp + xm + edges * h)
        for k, value in enumerate(out):
            coef[j - 1, k] = value


def advance(f, step_of_u, get, put, coef, first, count, fl, it):
    wide, deep = coef.shape[-2:]
    offset = coef.shape[0] // 2 - 1
    for j in range(first, first + count):
        on = (f == 0) & (it[2] <= step_of_u) & (it[0] == j)
        amp = jnp.where(on, fl[DOSE_AT], 0.0)
        for r in range(0, wide, ROWS):
            rows = pl.ds(r, ROWS)
            zp, zm, yp, ym, xp, xm, total = [coef[j + offset, k, rows, :] for k in range(7)]
            center = []
            for c in range(4):
                ref, index = get(c, j)
                center.append(ref[(*index, rows, slice(None))])
            for c in range(4):
                ref, index = get(c, j)
                v = center[c]
                ref_up, index_up = get(c, j + 1)
                ref_dn, index_dn = get(c, j - 1)
                flow = zp * pltpu.roll(v, deep - 1, 1) + zm * pltpu.roll(v, 1, 1)
                flow = flow + (yp * up(ref, index, r, ROWS) + ym * down(ref, index, r, ROWS))
                flow = flow + (
                    xp * ref_up[(*index_up, rows, slice(None))]
                    + xm * ref_dn[(*index_dn, rows, slice(None))]
                )
                flow = flow - total * v
                new = fl[TS_AT + c] * flow
                for d in range(4):
                    new = new + fl[A_AT + f * 16 + c * 4 + d] * center[d]
                if c == 0:
                    at = (
                        lax.broadcasted_iota(jnp.int32, (ROWS, deep), 0) + r
                    ) * deep + lax.broadcasted_iota(jnp.int32, (ROWS, deep), 1)
                    new = new + jnp.where(at == it[1], amp, 0.0)
                if j < 0:
                    new = new * fl[LO_AT]
                if j > 1:
                    new = new * fl[HI_AT]
                for out, index_out in put(c, j):
                    out[(*index_out, rows, slice(None))] = new


def two_steps(first_step, perm_at):
    def kernel(fl, it, own, low, high, plow, pmid, phigh, *rest):
        labels, rest = (rest[:1], rest[1:]) if first_step == 0 else ((), rest)
        mid, out, coef = rest[0], rest[1:-1], rest[-1]
        for ref in labels:
            out[0][16] = ref[1].astype(F32)
            out[1][16] = ref[0].astype(F32)
        planes = [plow[(*perm_at, 0)], plow[(*perm_at, 1)], pmid[0], pmid[1]]
        planes += [phigh[(*perm_at, 0)], phigh[(*perm_at, 1)]]
        face_weights(planes, coef)

        def field(f, carry):
            def source(c, j):
                k = f * 4 + c
                if first_step == 0:
                    if j < 0:
                        return low, (k, j + 2)
                    return (high, (k, j - 2)) if j > 1 else (own, (k, j))
                if j < 0:
                    return low, (2 * k + j + 2,)
                return (high, (2 * k + j - 2,)) if j > 1 else (own, (2 * k + j,))

            def middle(c, j):
                return [(mid, (f * 4 + c, j + 1))]

            def last(c, j):
                k = f * 4 + c
                return [(x, (2 * k + j,)) for x in out] if first_step == 0 else [(out[j], (k,))]

            advance(f, first_step, source, middle, coef, -1, 4, fl, it)
            advance(f, first_step + 1, lambda c, j: middle(c, j)[0], last, coef, 0, 2, fl, it)
            return carry

        lax.fori_loop(0, 2, field, 0)

    return kernel


def pieces(x):
    first = x.astype(jnp.bfloat16)
    rest = x - first.astype(F32)
    second = rest.astype(jnp.bfloat16)
    return first, second, (rest - second.astype(F32)).astype(jnp.bfloat16)


def gradient(fl, s0, low0, high0, t1, s2, low2, high2, t3, s4a, s4b, perm, labels, bins, out, fz, fy, fb, half):
    wide, deep = out.shape[-2:]

    def plane(stage, f, c, j):
        k = f * 4 + c
        if stage == 0:
            return s0, (k, j)
        if stage == 1:
            return t1, (k, j + 1)
        if stage == 3:
            return t3, (k, j + 1)
        if stage == 4:
            return (s4a, (k,)) if j == 0 else (s4b, (k,))
        if j < 0:
            return low2, (2 * k + 1,)
        if j > 1:
            return high2, (2 * k,)
        return s2, (2 * k + j,)

    for r in range(0, wide, ROWS):
        rows = pl.ds(r, ROWS)
        x_low = x_mid = x_high = half_low = half_high = jnp.zeros((ROWS, deep), F32)
        acc_z, acc_y, acc_b = [[jnp.zeros((ROWS, deep), F32)] * 2 for _ in range(3)]
        for n in range(STEPS):
            for c in range(4):
                def load(f, j):
                    ref, index = plane(n if f == 0 else STEPS - 1 - n, f, c, j)
                    return ref[(*index, rows, slice(None))]

                def load_up(f, j):
                    ref, index = plane(n if f == 0 else STEPS - 1 - n, f, c, j)
                    return up(ref, index, r, ROWS)

                weight = fl[S_AT + c]
                u = [load(0, 0), load(0, 1)]
                l = [load(1, 0), load(1, 1)]
                w = [l[0] * weight, l[1] * weight]
                for j in range(2):
                    acc_b[j] = acc_b[j] + w[j] * u[j]
                    acc_z[j] = acc_z[j] + (pltpu.roll(w[j], deep - 1, 1) - w[j]) * (
                        pltpu.roll(u[j], deep - 1, 1) - u[j]
                    )
                    acc_y[j] = acc_y[j] + (load_up(1, j) * weight - w[j]) * (load_up(0, j) - u[j])
                x_mid = x_mid + (w[1] - w[0]) * (u[1] - u[0])
                if 0 < n < STEPS - 1:
                    x_low = x_low + (load(1, -1) * weight - w[0]) * (load(0, -1) - u[0])
                    x_high = x_high + (load(1, 2) * weight - w[1]) * (load(0, 2) - u[1])
                elif n == 0:
                    half_low = half_low + w[0] * (u[0] - low0[c, 1, rows, :])
                    half_high = half_high + w[1] * (u[1] - high0[c, 0, rows, :])
                else:
                    half_low = half_low + (w[0] - weight * low0[4 + c, 1, rows, :]) * u[0]
                    half_high = half_high + (w[1] - weight * high0[4 + c, 0, rows, :]) * u[1]
        out[0, rows, :] = x_low + x_mid + half_low
        out[1, rows, :] = x_high + x_mid + half_high
        half[0, rows, :] = half_low
        half[1, rows, :] = half_high
        for j in range(2):
            fz[j, rows, :] = acc_z[j]
            fy[j, rows, :] = acc_y[j]
            fb[j, rows, :] = acc_b[j]
    row = lax.broadcasted_iota(jnp.int32, (wide, deep), 0)
    lane = lax.broadcasted_iota(jnp.int32, (wide, deep), 1)
    for j in range(2):
        b = fb[j]
        z, y = fz[j], fy[j]
        total = out[j] + jnp.where(lane == deep - 1, b, z)
        total = total + jnp.where(lane == 0, b, pltpu.roll(z, 1, 1))
        total = total + jnp.where(row == wide - 1, b, y)
        total = total + jnp.where(row == 0, b, pltpu.roll(y, 1, 0))
        out[j] = total

    def bin_rows(k, total):
        rows = pl.ds(pl.multiple_of(k * 8, 8), 8)
        cells = [(out[j, rows, :], perm[j, rows, :], labels[j, rows, :]) for j in range(2)]
        for j, far, names, at in ((0, low0, low2, 1), (1, high0, high2, 0)):
            cells.append((half[j, rows, :], far[8, at, rows, :], names[16, rows, :].astype(jnp.int32)))
        left, right = [], []
        for g, weight, label in cells:
            value = g * weight * fl[NORM_AT]
            coarse, fine = ((label >> 5) & 3) * 4 + (label >> 7), label & 31
            for i in range(8):
                hit = jnp.broadcast_to(coarse[i : i + 1], (16, deep)) == lax.broadcasted_iota(
                    jnp.int32, (16, deep), 0
                )
                left.append(jnp.where(hit, jnp.broadcast_to(value[i : i + 1], (16, deep)), 0.0))
                hit = jnp.broadcast_to(fine[i : i + 1], (32, deep)) == lax.broadcasted_iota(
                    jnp.int32, (32, deep), 0
                )
                right.append(jnp.where(hit, 1.0, 0.0).astype(jnp.bfloat16))
        return total + lax.dot_general(
            jnp.concatenate(pieces(jnp.concatenate(left, axis=1)), axis=0),
            jnp.concatenate(right, axis=1),
            (((1,), (1,)), ((), ())),
            preferred_element_type=F32,
        )

    total = lax.fori_loop(0, wide // 8, bin_rows, jnp.zeros((48, 32), F32))
    total = total[0:16] + total[16:32] + total[32:48]
    for k in range(4):
        bins[:, 32 * k : 32 * k + 32] = total[4 * k : 4 * k + 4]


def last_step(fl, it, low0, perm, high0, low4, s4a, s4b, high4, conc, sens, coef):
    face_weights([low0[8, 1], perm[0], perm[1], high0[8, 0]], coef)
    for f, out in ((0, conc), (1, sens)):
        def source(c, j):
            return (low4, s4a, s4b, high4)[j + 1], (f * 4 + c,)

        def target(c, j):
            return [(out, (c, j))]

        advance(f, STEPS - 1, source, target, coef, 0, 2, fl, it)


SMEM = pl.BlockSpec(memory_space=pltpu.SMEM)
VMEM = pl.BlockSpec(memory_space=pltpu.VMEM)


def call(kernel, ins, scalars, outs, scratch, name, flops):
    size = sum(math.prod(x.shape) for x in ins) + sum(math.prod(s) for s in outs)
    return pl.pallas_call(
        kernel,
        out_shape=[jax.ShapeDtypeStruct(s, F32) for s in outs],
        in_specs=[SMEM] * len(scalars) + [VMEM] * len(ins),
        out_specs=[VMEM] * len(outs),
        scratch_shapes=[pltpu.VMEM(s, F32) for s in scratch],
        compiler_params=pltpu.CompilerParams(vmem_limit_bytes=24 << 20),
        cost_estimate=pl.CostEstimate(flops=flops, bytes_accessed=4 * size, transcendentals=0),
        name=name,
    )(*scalars, *ins)


def neighbours(block_low, block_high):
    count = lax.axis_size("space")
    forward = [(i, i + 1) for i in range(count - 1)]
    backward = [(target, source) for source, target in forward]
    return lax.ppermute(block_high, "space", forward), lax.ppermute(block_low, "space", backward)


def gather(x, axis, groups):
    copies = jnp.broadcast_to(x[None], (len(groups[0]), *x.shape))
    return lax.all_to_all(copies, axis, 0, 0, axis_index_groups=groups, tiled=True)


def sum_over(x, axis, groups):
    return jnp.sum(gather(x, axis, groups), axis=0)


def on_device(
    initial,
    cotangent,
    permeability,
    labels,
    comp_scale,
    coupling_mask,
    coupling_rate,
    dose,
    inject_voxel,
    arrival,
):
    rows, wide, deep = permeability.shape
    spaces, exps = lax.axis_size("space"), lax.axis_size("exp")
    here = lax.axis_index("space")
    mixing = coupling(coupling_mask, coupling_rate)
    eye = jnp.eye(4, dtype=F32)
    norm = math.sqrt(rows * spaces * wide * deep * exps / LABELS)
    fl = jnp.concatenate(
        [
            (eye + TAU * mixing).reshape(-1),
            (eye + TAU * mixing.T).reshape(-1),
            TAU * comp_scale,
            comp_scale,
            jnp.stack([(here > 0).astype(F32), (here < spaces - 1).astype(F32)]),
            TAU * dose,
            jnp.full((1,), -0.5 * TAU / norm, F32),
        ]
    )
    voxel = inject_voxel[0]
    it = jnp.stack([voxel // (wide * deep) - here * rows, voxel % (wide * deep), arrival[0]])

    s0 = jnp.concatenate([initial[0], cotangent[0], permeability[None]], axis=0)
    low0, high0 = neighbours(s0, s0)
    plane = (8, wide, deep)
    coef = (4, 7, wide, deep)
    t1, s2, s2_back = call(
        two_steps(0, (8,)), [s0, low0, high0, low0, permeability, high0, labels], [fl, it],
        [(8, 4, wide, deep), (17, wide, deep), (17, wide, deep)], [coef], "steps_1_2", 20_000_000,
    )
    low2, high2 = neighbours(s2_back, s2)
    t3, s4a, s4b = call(
        two_steps(2, (8,)), [s2, low2, high2, low0, permeability, high0], [fl, it],
        [(8, 4, wide, deep), plane, plane], [coef], "steps_3_4", 20_000_000,
    )
    bins, = call(
        gradient, [s0, low0, high0, t1, s2, low2, high2, t3, s4a, s4b, permeability, labels], [fl],
        [(4, 128)], [(2, wide, deep)] * 5, "gradient", 20_000_000,
    )
    near = 4 if spaces % 4 == 0 else spaces
    bins = sum_over(bins, "space", [[g * near + i for i in range(near)] for g in range(spaces // near)])
    if spaces > near:
        bins = sum_over(bins, "space", [[g * near + i for g in range(spaces // near)] for i in range(near)])
    bins, last_low, last_high = lax.optimization_barrier((bins, s4a, s4b))
    low4, high4 = neighbours(last_low, last_high)
    conc, sens = call(
        last_step, [low0, permeability, high0, low4, s4a, s4b, high4], [fl, it],
        [(4, 2, wide, deep)] * 2, [(2, 7, wide, deep)], "step_5", 10_000_000,
    )
    got = gather(bins, "exp", [list(range(exps))])
    got, conc, sens = lax.optimization_barrier((got, conc, sens))
    bins = jnp.sum(got, axis=0)
    return conc[None], sens[None], bins.reshape(-1)


def solution(mesh):
    return jax.shard_map(
        on_device,
        mesh=mesh,
        in_specs=(
            P("exp", None, "space", None, None),
            P("exp", None, "space", None, None),
            P("space", None, None),
            P("space", None, None),
            P(),
            P(),
            P(),
            P("exp"),
            P("exp"),
            P("exp"),
        ),
        out_specs=(P("exp", None, "space", None, None), P("exp", None, "space", None, None), P()),
        check_vma=False,
    )
```

```python
import math

import jax
import jax.numpy as jnp
from jax import lax
from jax.experimental import pallas as pl
from jax.experimental.pallas import tpu as pltpu
from jax.sharding import PartitionSpec as P

STEPS = 5
LABELS = 512
TAU = 0.1
ROWS = 16
F32 = jnp.float32

A_AT, TS_AT, S_AT, LO_AT, HI_AT, DOSE_AT, NORM_AT = 0, 32, 36, 40, 41, 42, 43


def coupling(coupling_mask, coupling_rate):
    size = coupling_rate.shape[0]
    off = coupling_mask.astype(F32) * coupling_rate * (1.0 - jnp.eye(size, dtype=F32))
    return off - jnp.diag(jnp.sum(off, axis=1))


def up(ref, index, r, rows):
    if r + rows < ref.shape[-2]:
        return ref[(*index, pl.ds(r + 1, rows), slice(None))]
    return pltpu.roll(ref[(*index, pl.ds(r, rows), slice(None))], rows - 1, 0)


def down(ref, index, r, rows):
    if r > 0:
        return ref[(*index, pl.ds(r - 1, rows), slice(None))]
    return pltpu.roll(ref[(*index, pl.ds(r, rows), slice(None))], 1, 0)


def face_weights(planes, coef):
    wide, deep = coef.shape[-2:]
    row = lax.broadcasted_iota(jnp.int32, (wide, deep), 0)
    lane = lax.broadcasted_iota(jnp.int32, (wide, deep), 1)
    edges = (
        (row == 0).astype(F32)
        + (row == wide - 1).astype(F32)
        + (lane == 0).astype(F32)
        + (lane == deep - 1).astype(F32)
    )
    half = [0.5 * p for p in planes]
    for j in range(1, len(planes) - 1):
        h = half[j]
        zp = jnp.where(lane == deep - 1, 0.0, h + pltpu.roll(h, deep - 1, 1))
        yp = jnp.where(row == wide - 1, 0.0, h + pltpu.roll(h, wide - 1, 0))
        zm = pltpu.roll(zp, 1, 1)
        ym = pltpu.roll(yp, 1, 0)
        xp = h + half[j + 1]
        xm = h + half[j - 1]
        out = (zp, zm, yp, ym, xp, xm, zp + zm + yp + ym + xp + xm + edges * h)
        for k, value in enumerate(out):
            coef[j - 1, k] = value


def advance(f, step_of_u, get, put, coef, first, count, fl, it):
    wide, deep = coef.shape[-2:]
    offset = coef.shape[0] // 2 - 1
    for j in range(first, first + count):
        on = (f == 0) & (it[2] <= step_of_u) & (it[0] == j)
        amp = jnp.where(on, fl[DOSE_AT], 0.0)
        for r in range(0, wide, ROWS):
            rows = pl.ds(r, ROWS)
            zp, zm, yp, ym, xp, xm, total = [coef[j + offset, k, rows, :] for k in range(7)]
            center = []
            for c in range(4):
                ref, index = get(c, j)
                center.append(ref[(*index, rows, slice(None))])
            for c in range(4):
                ref, index = get(c, j)
                v = center[c]
                ref_up, index_up = get(c, j + 1)
                ref_dn, index_dn = get(c, j - 1)
                flow = zp * pltpu.roll(v, deep - 1, 1) + zm * pltpu.roll(v, 1, 1)
                flow = flow + (yp * up(ref, index, r, ROWS) + ym * down(ref, index, r, ROWS))
                flow = flow + (
                    xp * ref_up[(*index_up, rows, slice(None))]
                    + xm * ref_dn[(*index_dn, rows, slice(None))]
                )
                flow = flow - total * v
                new = fl[TS_AT + c] * flow
                for d in range(4):
                    new = new + fl[A_AT + f * 16 + c * 4 + d] * center[d]
                if c == 0:
                    at = (
                        lax.broadcasted_iota(jnp.int32, (ROWS, deep), 0) + r
                    ) * deep + lax.broadcasted_iota(jnp.int32, (ROWS, deep), 1)
                    new = new + jnp.where(at == it[1], amp, 0.0)
                if j < 0:
                    new = new * fl[LO_AT]
                if j > 1:
                    new = new * fl[HI_AT]
                for out, index_out in put(c, j):
                    out[(*index_out, rows, slice(None))] = new


def two_steps(first_step):
    def kernel(fl, it, own, low, high, *rest):
        if first_step == 0:
            labels, pmid, mid, *out, coef = rest
            out[0][16] = labels[1].astype(F32)
            out[1][16] = labels[0].astype(F32)
            planes = [low[8, 0], low[8, 1], pmid[0], pmid[1], high[8, 0], high[8, 1]]
            face_weights(planes, coef)
        else:
            coef, mid, *out = rest

        def field(f, carry):
            def source(c, j):
                k = f * 4 + c
                if first_step == 0:
                    if j < 0:
                        return low, (k, j + 2)
                    return (high, (k, j - 2)) if j > 1 else (own, (k, j))
                if j < 0:
                    return low, (2 * k + j + 2,)
                return (high, (2 * k + j - 2,)) if j > 1 else (own, (2 * k + j,))

            def middle(c, j):
                return [(mid, (f * 4 + c, j + 1))]

            def last(c, j):
                k = f * 4 + c
                return [(x, (2 * k + j,)) for x in out] if first_step == 0 else [(out[j], (k,))]

            advance(f, first_step, source, middle, coef, -1, 4, fl, it)
            advance(f, first_step + 1, lambda c, j: middle(c, j)[0], last, coef, 0, 2, fl, it)
            return carry

        lax.fori_loop(0, 2, field, 0)

    return kernel


def pieces(x):
    first = x.astype(jnp.bfloat16)
    rest = x - first.astype(F32)
    second = rest.astype(jnp.bfloat16)
    return first, second, (rest - second.astype(F32)).astype(jnp.bfloat16)


def gradient(fl, s0, low0, high0, t1, s2, low2, high2, t3, s4a, s4b, perm, labels, bins, out, fz, fy, fb, half):
    wide, deep = out.shape[-2:]

    def plane(stage, f, c, j):
        k = f * 4 + c
        if stage == 0:
            return s0, (k, j)
        if stage == 1:
            return t1, (k, j + 1)
        if stage == 3:
            return t3, (k, j + 1)
        if stage == 4:
            return (s4a, (k,)) if j == 0 else (s4b, (k,))
        if j < 0:
            return low2, (2 * k + 1,)
        if j > 1:
            return high2, (2 * k,)
        return s2, (2 * k + j,)

    for r in range(0, wide, ROWS):
        rows = pl.ds(r, ROWS)
        x_low = x_mid = x_high = half_low = half_high = jnp.zeros((ROWS, deep), F32)
        acc_z, acc_y, acc_b = [[jnp.zeros((ROWS, deep), F32)] * 2 for _ in range(3)]
        for n in range(STEPS):
            for c in range(4):
                def load(f, j):
                    ref, index = plane(n if f == 0 else STEPS - 1 - n, f, c, j)
                    return ref[(*index, rows, slice(None))]

                def load_up(f, j):
                    ref, index = plane(n if f == 0 else STEPS - 1 - n, f, c, j)
                    return up(ref, index, r, ROWS)

                weight = fl[S_AT + c]
                u = [load(0, 0), load(0, 1)]
                l = [load(1, 0), load(1, 1)]
                w = [l[0] * weight, l[1] * weight]
                for j in range(2):
                    acc_b[j] = acc_b[j] + w[j] * u[j]
                    acc_z[j] = acc_z[j] + (pltpu.roll(w[j], deep - 1, 1) - w[j]) * (
                        pltpu.roll(u[j], deep - 1, 1) - u[j]
                    )
                    acc_y[j] = acc_y[j] + (load_up(1, j) * weight - w[j]) * (load_up(0, j) - u[j])
                x_mid = x_mid + (w[1] - w[0]) * (u[1] - u[0])
                if 0 < n < STEPS - 1:
                    x_low = x_low + (load(1, -1) * weight - w[0]) * (load(0, -1) - u[0])
                    x_high = x_high + (load(1, 2) * weight - w[1]) * (load(0, 2) - u[1])
                elif n == 0:
                    half_low = half_low + w[0] * (u[0] - low0[c, 1, rows, :])
                    half_high = half_high + w[1] * (u[1] - high0[c, 0, rows, :])
                else:
                    half_low = half_low + (w[0] - weight * low0[4 + c, 1, rows, :]) * u[0]
                    half_high = half_high + (w[1] - weight * high0[4 + c, 0, rows, :]) * u[1]
        out[0, rows, :] = x_low + x_mid + half_low
        out[1, rows, :] = x_high + x_mid + half_high
        half[0, rows, :] = half_low
        half[1, rows, :] = half_high
        for j in range(2):
            fz[j, rows, :] = acc_z[j]
            fy[j, rows, :] = acc_y[j]
            fb[j, rows, :] = acc_b[j]
    row = lax.broadcasted_iota(jnp.int32, (wide, deep), 0)
    lane = lax.broadcasted_iota(jnp.int32, (wide, deep), 1)
    for j in range(2):
        b = fb[j]
        z, y = fz[j], fy[j]
        total = out[j] + jnp.where(lane == deep - 1, b, z)
        total = total + jnp.where(lane == 0, b, pltpu.roll(z, 1, 1))
        total = total + jnp.where(row == wide - 1, b, y)
        total = total + jnp.where(row == 0, b, pltpu.roll(y, 1, 0))
        out[j] = total

    def bin_rows(k, total):
        rows = pl.ds(pl.multiple_of(k * 8, 8), 8)
        cells = [(out[j, rows, :], perm[j, rows, :], labels[j, rows, :]) for j in range(2)]
        for j, far, names, at in ((0, low0, low2, 1), (1, high0, high2, 0)):
            cells.append((half[j, rows, :], far[8, at, rows, :], names[16, rows, :].astype(jnp.int32)))
        left, right = [], []
        for g, weight, label in cells:
            value = g * weight * fl[NORM_AT]
            coarse, fine = ((label >> 5) & 3) * 4 + (label >> 7), label & 31
            for i in range(8):
                hit = jnp.broadcast_to(coarse[i : i + 1], (16, deep)) == lax.broadcasted_iota(
                    jnp.int32, (16, deep), 0
                )
                left.append(jnp.where(hit, jnp.broadcast_to(value[i : i + 1], (16, deep)), 0.0))
                hit = jnp.broadcast_to(fine[i : i + 1], (32, deep)) == lax.broadcasted_iota(
                    jnp.int32, (32, deep), 0
                )
                right.append(jnp.where(hit, 1.0, 0.0).astype(jnp.bfloat16))
        return total + lax.dot_general(
            jnp.concatenate(pieces(jnp.concatenate(left, axis=1)), axis=0),
            jnp.concatenate(right, axis=1),
            (((1,), (1,)), ((), ())),
            preferred_element_type=F32,
        )

    total = lax.fori_loop(0, wide // 8, bin_rows, jnp.zeros((48, 32), F32))
    total = total[0:16] + total[16:32] + total[32:48]
    for k in range(4):
        bins[:, 32 * k : 32 * k + 32] = total[4 * k : 4 * k + 4]


def last_step(fl, it, low0, perm, high0, low4, s4a, s4b, high4, conc, sens, coef):
    face_weights([low0[8, 1], perm[0], perm[1], high0[8, 0]], coef)
    for f, out in ((0, conc), (1, sens)):
        def source(c, j):
            return (low4, s4a, s4b, high4)[j + 1], (f * 4 + c,)

        def target(c, j):
            return [(out, (c, j))]

        advance(f, STEPS - 1, source, target, coef, 0, 2, fl, it)


SMEM = pl.BlockSpec(memory_space=pltpu.SMEM)
VMEM = pl.BlockSpec(memory_space=pltpu.VMEM)


def call(kernel, ins, scalars, outs, scratch, name, flops):
    size = sum(math.prod(x.shape) for x in ins) + sum(math.prod(s) for s in outs)
    return pl.pallas_call(
        kernel,
        out_shape=[jax.ShapeDtypeStruct(s, F32) for s in outs],
        in_specs=[SMEM] * len(scalars) + [VMEM] * len(ins),
        out_specs=[VMEM] * len(outs),
        scratch_shapes=[pltpu.VMEM(s, F32) for s in scratch],
        compiler_params=pltpu.CompilerParams(vmem_limit_bytes=24 << 20),
        cost_estimate=pl.CostEstimate(flops=flops, bytes_accessed=4 * size, transcendentals=0),
        name=name,
    )(*scalars, *ins)


def neighbours(block_low, block_high):
    count = lax.axis_size("space")
    forward = [(i, i + 1) for i in range(count - 1)]
    backward = [(target, source) for source, target in forward]
    return lax.ppermute(block_high, "space", forward), lax.ppermute(block_low, "space", backward)


def gather(x, axis, groups):
    copies = jnp.broadcast_to(x[None], (len(groups[0]), *x.shape))
    return lax.all_to_all(copies, axis, 0, 0, axis_index_groups=groups, tiled=True)


def sum_over(x, axis, groups):
    return jnp.sum(gather(x, axis, groups), axis=0)


def on_device(
    initial,
    cotangent,
    permeability,
    labels,
    comp_scale,
    coupling_mask,
    coupling_rate,
    dose,
    inject_voxel,
    arrival,
):
    rows, wide, deep = permeability.shape
    spaces, exps = lax.axis_size("space"), lax.axis_size("exp")
    here = lax.axis_index("space")
    mixing = coupling(coupling_mask, coupling_rate)
    eye = jnp.eye(4, dtype=F32)
    norm = math.sqrt(rows * spaces * wide * deep * exps / LABELS)
    fl = jnp.concatenate(
        [
            (eye + TAU * mixing).reshape(-1),
            (eye + TAU * mixing.T).reshape(-1),
            TAU * comp_scale,
            comp_scale,
            jnp.stack([(here > 0).astype(F32), (here < spaces - 1).astype(F32)]),
            TAU * dose,
            jnp.full((1,), -0.5 * TAU / norm, F32),
        ]
    )
    voxel = inject_voxel[0]
    it = jnp.stack([voxel // (wide * deep) - here * rows, voxel % (wide * deep), arrival[0]])

    s0 = jnp.concatenate([initial[0], cotangent[0], permeability[None]], axis=0)
    low0, high0 = neighbours(s0, s0)
    plane = (8, wide, deep)
    coef = (4, 7, wide, deep)
    t1, s2, s2_back, weights = call(
        two_steps(0), [s0, low0, high0, labels, permeability], [fl, it],
        [(8, 4, wide, deep), (17, wide, deep), (17, wide, deep), coef], [], "steps_1_2", 20_000_000,
    )
    low2, high2 = neighbours(s2_back, s2)
    t3, s4a, s4b = call(
        two_steps(2), [s2, low2, high2, weights], [fl, it],
        [(8, 4, wide, deep), plane, plane], [], "steps_3_4", 20_000_000,
    )
    bins, = call(
        gradient, [s0, low0, high0, t1, s2, low2, high2, t3, s4a, s4b, permeability, labels], [fl],
        [(4, 128)], [(2, wide, deep)] * 5, "gradient", 20_000_000,
    )
    near = 4 if spaces % 4 == 0 else spaces
    bins = sum_over(bins, "space", [[g * near + i for i in range(near)] for g in range(spaces // near)])
    if spaces > near:
        bins = sum_over(bins, "space", [[g * near + i for g in range(spaces // near)] for i in range(near)])
    bins, last_low, last_high = lax.optimization_barrier((bins, s4a, s4b))
    low4, high4 = neighbours(last_low, last_high)
    conc, sens = call(
        last_step, [low0, permeability, high0, low4, s4a, s4b, high4], [fl, it],
        [(4, 2, wide, deep)] * 2, [(2, 7, wide, deep)], "step_5", 10_000_000,
    )
    got = gather(bins, "exp", [list(range(exps))])
    got, conc, sens = lax.optimization_barrier((got, conc, sens))
    bins = jnp.sum(got, axis=0)
    return conc[None], sens[None], bins.reshape(-1)


def solution(mesh):
    return jax.shard_map(
        on_device,
        mesh=mesh,
        in_specs=(
            P("exp", None, "space", None, None),
            P("exp", None, "space", None, None),
            P("space", None, None),
            P("space", None, None),
            P(),
            P(),
            P(),
            P("exp"),
            P("exp"),
            P("exp"),
        ),
        out_specs=(P("exp", None, "space", None, None), P("exp", None, "space", None, None), P()),
        check_vma=False,
    )
```

```python
import math

import jax
import jax.numpy as jnp
from jax import lax
from jax.experimental import pallas as pl
from jax.experimental.pallas import tpu as pltpu
from jax.sharding import PartitionSpec as P

STEPS = 5
LABELS = 512
TAU = 0.1
ROWS = 8
F32 = jnp.float32

A_AT, TS_AT, S_AT, LO_AT, HI_AT, DOSE_AT, NORM_AT = 0, 32, 36, 40, 41, 42, 43


def coupling(coupling_mask, coupling_rate):
    size = coupling_rate.shape[0]
    off = coupling_mask.astype(F32) * coupling_rate * (1.0 - jnp.eye(size, dtype=F32))
    return off - jnp.diag(jnp.sum(off, axis=1))


def up(ref, index, r, rows):
    if r + rows < ref.shape[-2]:
        return ref[(*index, pl.ds(r + 1, rows), slice(None))]
    return pltpu.roll(ref[(*index, pl.ds(r, rows), slice(None))], rows - 1, 0)


def down(ref, index, r, rows):
    if r > 0:
        return ref[(*index, pl.ds(r - 1, rows), slice(None))]
    return pltpu.roll(ref[(*index, pl.ds(r, rows), slice(None))], 1, 0)


def face_weights(planes, coef):
    wide, deep = coef.shape[-2:]
    row = lax.broadcasted_iota(jnp.int32, (wide, deep), 0)
    lane = lax.broadcasted_iota(jnp.int32, (wide, deep), 1)
    edges = (
        (row == 0).astype(F32)
        + (row == wide - 1).astype(F32)
        + (lane == 0).astype(F32)
        + (lane == deep - 1).astype(F32)
    )
    half = [0.5 * p for p in planes]
    for j in range(1, len(planes) - 1):
        h = half[j]
        zp = jnp.where(lane == deep - 1, 0.0, h + pltpu.roll(h, deep - 1, 1))
        yp = jnp.where(row == wide - 1, 0.0, h + pltpu.roll(h, wide - 1, 0))
        zm = pltpu.roll(zp, 1, 1)
        ym = pltpu.roll(yp, 1, 0)
        xp = h + half[j + 1]
        xm = h + half[j - 1]
        out = (zp, zm, yp, ym, xp, xm, zp + zm + yp + ym + xp + xm + edges * h)
        for k, value in enumerate(out):
            coef[j - 1, k] = value


def advance(f, step_of_u, get, put, coef, first, count, fl, it):
    wide, deep = coef.shape[-2:]
    offset = coef.shape[0] // 2 - 1
    for j in range(first, first + count):
        on = (f == 0) & (it[2] <= step_of_u) & (it[0] == j)
        amp = jnp.where(on, fl[DOSE_AT], 0.0)
        for r in range(0, wide, ROWS):
            rows = pl.ds(r, ROWS)
            zp, zm, yp, ym, xp, xm, total = [coef[j + offset, k, rows, :] for k in range(7)]
            center = []
            for c in range(4):
                ref, index = get(c, j)
                center.append(ref[(*index, rows, slice(None))])
            for c in range(4):
                ref, index = get(c, j)
                v = center[c]
                ref_up, index_up = get(c, j + 1)
                ref_dn, index_dn = get(c, j - 1)
                flow = zp * pltpu.roll(v, deep - 1, 1) + zm * pltpu.roll(v, 1, 1)
                flow = flow + (yp * up(ref, index, r, ROWS) + ym * down(ref, index, r, ROWS))
                flow = flow + (
                    xp * ref_up[(*index_up, rows, slice(None))]
                    + xm * ref_dn[(*index_dn, rows, slice(None))]
                )
                flow = flow - total * v
                new = fl[TS_AT + c] * flow
                for d in range(4):
                    new = new + fl[A_AT + f * 16 + c * 4 + d] * center[d]
                if c == 0:
                    at = (
                        lax.broadcasted_iota(jnp.int32, (ROWS, deep), 0) + r
                    ) * deep + lax.broadcasted_iota(jnp.int32, (ROWS, deep), 1)
                    new = new + jnp.where(at == it[1], amp, 0.0)
                if j < 0:
                    new = new * fl[LO_AT]
                if j > 1:
                    new = new * fl[HI_AT]
                for out, index_out in put(c, j):
                    out[(*index_out, rows, slice(None))] = new


def two_steps(first_step):
    def kernel(fl, it, own, low, high, *rest):
        if first_step == 0:
            labels, pmid, mid, *out, coef = rest
            out[0][16] = labels[1].astype(F32)
            out[1][16] = labels[0].astype(F32)
            planes = [low[8, 0], low[8, 1], pmid[0], pmid[1], high[8, 0], high[8, 1]]
            face_weights(planes, coef)
        else:
            coef, mid, *out = rest

        def field(f, carry):
            def source(c, j):
                k = f * 4 + c
                if first_step == 0:
                    if j < 0:
                        return low, (k, j + 2)
                    return (high, (k, j - 2)) if j > 1 else (own, (k, j))
                if j < 0:
                    return low, (2 * k + j + 2,)
                return (high, (2 * k + j - 2,)) if j > 1 else (own, (2 * k + j,))

            def middle(c, j):
                return [(mid, (f * 4 + c, j + 1))]

            def last(c, j):
                k = f * 4 + c
                return [(x, (2 * k + j,)) for x in out] if first_step == 0 else [(out[j], (k,))]

            advance(f, first_step, source, middle, coef, -1, 4, fl, it)
            advance(f, first_step + 1, lambda c, j: middle(c, j)[0], last, coef, 0, 2, fl, it)
            return carry

        lax.fori_loop(0, 2, field, 0)

    return kernel


def pieces(x):
    first = x.astype(jnp.bfloat16)
    rest = x - first.astype(F32)
    second = rest.astype(jnp.bfloat16)
    return first, second, (rest - second.astype(F32)).astype(jnp.bfloat16)


def gradient(fl, s0, low0, high0, t1, s2, low2, high2, t3, s4a, s4b, perm, labels, bins, out, fz, fy, fb, half):
    wide, deep = out.shape[-2:]

    def plane(stage, f, c, j):
        k = f * 4 + c
        if stage == 0:
            return s0, (k, j)
        if stage == 1:
            return t1, (k, j + 1)
        if stage == 3:
            return t3, (k, j + 1)
        if stage == 4:
            return (s4a, (k,)) if j == 0 else (s4b, (k,))
        if j < 0:
            return low2, (2 * k + 1,)
        if j > 1:
            return high2, (2 * k,)
        return s2, (2 * k + j,)

    for r in range(0, wide, ROWS):
        rows = pl.ds(r, ROWS)
        x_low = x_mid = x_high = half_low = half_high = jnp.zeros((ROWS, deep), F32)
        acc_z, acc_y, acc_b = [[jnp.zeros((ROWS, deep), F32)] * 2 for _ in range(3)]
        for n in range(STEPS):
            for c in range(4):
                def load(f, j):
                    ref, index = plane(n if f == 0 else STEPS - 1 - n, f, c, j)
                    return ref[(*index, rows, slice(None))]

                def load_up(f, j):
                    ref, index = plane(n if f == 0 else STEPS - 1 - n, f, c, j)
                    return up(ref, index, r, ROWS)

                weight = fl[S_AT + c]
                u = [load(0, 0), load(0, 1)]
                l = [load(1, 0), load(1, 1)]
                w = [l[0] * weight, l[1] * weight]
                for j in range(2):
                    acc_b[j] = acc_b[j] + w[j] * u[j]
                    acc_z[j] = acc_z[j] + (pltpu.roll(w[j], deep - 1, 1) - w[j]) * (
                        pltpu.roll(u[j], deep - 1, 1) - u[j]
                    )
                    acc_y[j] = acc_y[j] + (load_up(1, j) * weight - w[j]) * (load_up(0, j) - u[j])
                x_mid = x_mid + (w[1] - w[0]) * (u[1] - u[0])
                if 0 < n < STEPS - 1:
                    x_low = x_low + (load(1, -1) * weight - w[0]) * (load(0, -1) - u[0])
                    x_high = x_high + (load(1, 2) * weight - w[1]) * (load(0, 2) - u[1])
                elif n == 0:
                    half_low = half_low + w[0] * (u[0] - low0[c, 1, rows, :])
                    half_high = half_high + w[1] * (u[1] - high0[c, 0, rows, :])
                else:
                    half_low = half_low + (w[0] - weight * low0[4 + c, 1, rows, :]) * u[0]
                    half_high = half_high + (w[1] - weight * high0[4 + c, 0, rows, :]) * u[1]
        out[0, rows, :] = x_low + x_mid + half_low
        out[1, rows, :] = x_high + x_mid + half_high
        half[0, rows, :] = half_low
        half[1, rows, :] = half_high
        for j in range(2):
            fz[j, rows, :] = acc_z[j]
            fy[j, rows, :] = acc_y[j]
            fb[j, rows, :] = acc_b[j]
    row = lax.broadcasted_iota(jnp.int32, (wide, deep), 0)
    lane = lax.broadcasted_iota(jnp.int32, (wide, deep), 1)
    for j in range(2):
        b = fb[j]
        z, y = fz[j], fy[j]
        total = out[j] + jnp.where(lane == deep - 1, b, z)
        total = total + jnp.where(lane == 0, b, pltpu.roll(z, 1, 1))
        total = total + jnp.where(row == wide - 1, b, y)
        total = total + jnp.where(row == 0, b, pltpu.roll(y, 1, 0))
        out[j] = total

    def bin_rows(k, total):
        rows = pl.ds(pl.multiple_of(k * 8, 8), 8)
        cells = [(out[j, rows, :], perm[j, rows, :], labels[j, rows, :]) for j in range(2)]
        for j, far, names, at in ((0, low0, low2, 1), (1, high0, high2, 0)):
            cells.append((half[j, rows, :], far[8, at, rows, :], names[16, rows, :].astype(jnp.int32)))
        left, right = [], []
        for g, weight, label in cells:
            value = g * weight * fl[NORM_AT]
            coarse, fine = ((label >> 5) & 3) * 4 + (label >> 7), label & 31
            for i in range(8):
                hit = jnp.broadcast_to(coarse[i : i + 1], (16, deep)) == lax.broadcasted_iota(
                    jnp.int32, (16, deep), 0
                )
                left.append(jnp.where(hit, jnp.broadcast_to(value[i : i + 1], (16, deep)), 0.0))
                hit = jnp.broadcast_to(fine[i : i + 1], (32, deep)) == lax.broadcasted_iota(
                    jnp.int32, (32, deep), 0
                )
                right.append(jnp.where(hit, 1.0, 0.0).astype(jnp.bfloat16))
        return total + lax.dot_general(
            jnp.concatenate(pieces(jnp.concatenate(left, axis=1)), axis=0),
            jnp.concatenate(right, axis=1),
            (((1,), (1,)), ((), ())),
            preferred_element_type=F32,
        )

    total = lax.fori_loop(0, wide // 8, bin_rows, jnp.zeros((48, 32), F32))
    total = total[0:16] + total[16:32] + total[32:48]
    for k in range(4):
        bins[:, 32 * k : 32 * k + 32] = total[4 * k : 4 * k + 4]


def last_step(fl, it, low0, perm, high0, low4, s4a, s4b, high4, conc, sens, coef):
    face_weights([low0[8, 1], perm[0], perm[1], high0[8, 0]], coef)
    for f, out in ((0, conc), (1, sens)):
        def source(c, j):
            return (low4, s4a, s4b, high4)[j + 1], (f * 4 + c,)

        def target(c, j):
            return [(out, (c, j))]

        advance(f, STEPS - 1, source, target, coef, 0, 2, fl, it)


SMEM = pl.BlockSpec(memory_space=pltpu.SMEM)
VMEM = pl.BlockSpec(memory_space=pltpu.VMEM)


def call(kernel, ins, scalars, outs, scratch, name, flops):
    size = sum(math.prod(x.shape) for x in ins) + sum(math.prod(s) for s in outs)
    return pl.pallas_call(
        kernel,
        out_shape=[jax.ShapeDtypeStruct(s, F32) for s in outs],
        in_specs=[SMEM] * len(scalars) + [VMEM] * len(ins),
        out_specs=[VMEM] * len(outs),
        scratch_shapes=[pltpu.VMEM(s, F32) for s in scratch],
        compiler_params=pltpu.CompilerParams(vmem_limit_bytes=24 << 20),
        cost_estimate=pl.CostEstimate(flops=flops, bytes_accessed=4 * size, transcendentals=0),
        name=name,
    )(*scalars, *ins)


def neighbours(block_low, block_high):
    count = lax.axis_size("space")
    forward = [(i, i + 1) for i in range(count - 1)]
    backward = [(target, source) for source, target in forward]
    return lax.ppermute(block_high, "space", forward), lax.ppermute(block_low, "space", backward)


def gather(x, axis, groups):
    copies = jnp.broadcast_to(x[None], (len(groups[0]), *x.shape))
    return lax.all_to_all(copies, axis, 0, 0, axis_index_groups=groups, tiled=True)


def sum_over(x, axis, groups):
    return jnp.sum(gather(x, axis, groups), axis=0)


def on_device(
    initial,
    cotangent,
    permeability,
    labels,
    comp_scale,
    coupling_mask,
    coupling_rate,
    dose,
    inject_voxel,
    arrival,
):
    rows, wide, deep = permeability.shape
    spaces, exps = lax.axis_size("space"), lax.axis_size("exp")
    here = lax.axis_index("space")
    mixing = coupling(coupling_mask, coupling_rate)
    eye = jnp.eye(4, dtype=F32)
    norm = math.sqrt(rows * spaces * wide * deep * exps / LABELS)
    fl = jnp.concatenate(
        [
            (eye + TAU * mixing).reshape(-1),
            (eye + TAU * mixing.T).reshape(-1),
            TAU * comp_scale,
            comp_scale,
            jnp.stack([(here > 0).astype(F32), (here < spaces - 1).astype(F32)]),
            TAU * dose,
            jnp.full((1,), -0.5 * TAU / norm, F32),
        ]
    )
    voxel = inject_voxel[0]
    it = jnp.stack([voxel // (wide * deep) - here * rows, voxel % (wide * deep), arrival[0]])

    s0 = jnp.concatenate([initial[0], cotangent[0], permeability[None]], axis=0)
    low0, high0 = neighbours(s0, s0)
    plane = (8, wide, deep)
    coef = (4, 7, wide, deep)
    t1, s2, s2_back, weights = call(
        two_steps(0), [s0, low0, high0, labels, permeability], [fl, it],
        [(8, 4, wide, deep), (17, wide, deep), (17, wide, deep), coef], [], "steps_1_2", 20_000_000,
    )
    low2, high2 = neighbours(s2_back, s2)
    t3, s4a, s4b = call(
        two_steps(2), [s2, low2, high2, weights], [fl, it],
        [(8, 4, wide, deep), plane, plane], [], "steps_3_4", 20_000_000,
    )
    bins, = call(
        gradient, [s0, low0, high0, t1, s2, low2, high2, t3, s4a, s4b, permeability, labels], [fl],
        [(4, 128)], [(2, wide, deep)] * 5, "gradient", 20_000_000,
    )
    near = 4 if spaces % 4 == 0 else spaces
    bins = sum_over(bins, "space", [[g * near + i for i in range(near)] for g in range(spaces // near)])
    if spaces > near:
        bins = sum_over(bins, "space", [[g * near + i for g in range(spaces // near)] for i in range(near)])
    bins, last_low, last_high = lax.optimization_barrier((bins, s4a, s4b))
    low4, high4 = neighbours(last_low, last_high)
    conc, sens = call(
        last_step, [low0, permeability, high0, low4, s4a, s4b, high4], [fl, it],
        [(4, 2, wide, deep)] * 2, [(2, 7, wide, deep)], "step_5", 10_000_000,
    )
    got = gather(bins, "exp", [list(range(exps))])
    got, conc, sens = lax.optimization_barrier((got, conc, sens))
    bins = jnp.sum(got, axis=0)
    return conc[None], sens[None], bins.reshape(-1)


def solution(mesh):
    return jax.shard_map(
        on_device,
        mesh=mesh,
        in_specs=(
            P("exp", None, "space", None, None),
            P("exp", None, "space", None, None),
            P("space", None, None),
            P("space", None, None),
            P(),
            P(),
            P(),
            P("exp"),
            P("exp"),
            P("exp"),
        ),
        out_specs=(P("exp", None, "space", None, None), P("exp", None, "space", None, None), P()),
        check_vma=False,
    )
```
